32 devices in a mesh: tm: 4 (over y, core), tile: 8 (over z, x).
Axes of the slice: x: 2, y: 2, z: 4, core: 2. Of those that a mesh axis runs over, the one named last changes fastest.
Arguments:
- basis_fields: bfloat16 [4, 3, 256, 64, 256], P('tm', None, None, 'tile'), may hold values from -0.5 to 0.5
- mean_depth: float32 [64, 256], P('tile'), may hold values from 0.5 to 1.9
- obs_cells: int32 [4, 2048], P('tm', 'tile'), may hold values from 0 to 16383, as said below
- obs_fields: int32 [4, 2048], P('tm', 'tile'), may hold values from 0 to 2
- obs_weight: float32 [4, 2048], P('tm', 'tile'), may hold values from 0.05 to 0.5
- innovation: float32 [4, 2048], P('tm', 'tile'), may hold values from -6 to 6
- transition: float32 [256, 256], replicated, may hold values from -1 to 1
- model_error: float32 [256], replicated, may hold values from 0.2 to 1
Outputs:
- reduced_mean: float32 [4, 256], P('tm')
- increments: float32 [4, 3, 64, 256], P('tm', None, 'tile')
The draws below stay inside these ranges and needn't reach their ends.
Inputs may be any that keep to these rules, and one draw needn't show every extreme that they name: obs_cells[k, o] lies in grid rows (o // 256) * 8 to (o // 256) * 8 + 7. `obs_fields`: 0 is height, 1 eastward velocity, 2 northward velocity.
All inputs are finite; a program needn't handle non-finite values.
Results may differ from the reference program's by a relative error of at most 0.0003.
Values sent between devices are 32-bit elements; how exact they have to be, the bound alone decides.
No kernel may reach another device: no remote copies, remote signals or barrier semaphores. Data moves between devices by JAX's collectives and lax.ppermute only.
A program may use at most 64 MiB of HBM per device.

```python
import math
import jax
import jax.numpy as jnp
from jax import lax

R = 256
SY = 8
NX = 256
OBS_DEV = 256
STEPS = 4
SUBWIN = 4
NY = 64
OBS = 2048


def draw_obs_cells(key, part):
    offsets = jax.random.randint(key, (SUBWIN, OBS), 0, SY * NX, dtype=jnp.int32)
    offsets = offsets.at[0, 0].set(0).at[SUBWIN - 1, OBS - 1].set(SY * NX - 1)
    block_owner = jnp.arange(OBS, dtype=jnp.int32) // OBS_DEV
    return block_owner[None, :] * (SY * NX) + offsets


def draw_transition(key, part):
    random_part = jnp.clip(jax.random.normal(key, (R, R), jnp.float32), -6.0, 6.0)
    diagonal = 0.6
    return diagonal * jnp.eye(R, dtype=jnp.float32) + 0.25 / R ** 0.5 * random_part


def touch_ends(array, key, smallest, top_value):
    longest = array.shape.index(max(array.shape))
    spots = []
    for shift in (0, 1):
        where = [jax.random.randint(jax.random.fold_in(key, axis), (), 0, length) for axis, length in enumerate(array.shape)]
        where[longest] = (where[longest] + shift) % array.shape[longest]
        spots.append(tuple(where))
    return array.at[spots[0]].set(smallest).at[spots[1]].set(top_value)


def level_of(rng, dims, split, low, largest):
    def one(dim, parts):
        heights = jax.random.uniform(jax.random.fold_in(jax.random.fold_in(rng, 6), dim), (parts,), jnp.float32, low / len(split), largest / len(split))
        return jnp.repeat(jnp.exp(heights), dims[dim] // parts).reshape((-1,) + (1,) * (len(dims) - dim - 1))

    factor_of = one(*split[0])
    for cut in split[1:]:
        factor_of = factor_of * one(*cut)
    return factor_of


def bell_draw(stream_key, shape, spread, bound, shards=(), held_as=jnp.bfloat16):
    level = level_of(stream_key, shape, shards, -0.22, 0.18) if shards else 1.0
    result = jax.random.normal(stream_key, shape, jnp.float32) * spread * level
    return jnp.minimum(jnp.maximum(result, -bound), bound).astype(held_as)


def setup_inputs(seed: int = 0) -> dict:
    streams_of = jax.random.split(jax.random.key(seed), 9)
    basis_fields = bell_draw(streams_of[0], (SUBWIN, 3, R, NY, NX), 0.0625, 0.5, ((0, 4), (3, 8)))
    mean_depth = jnp.clip(jnp.exp(math.log(1.9) - 1.3350011 * jax.random.uniform(streams_of[1], (NY, NX), jnp.float32) ** level_of(streams_of[1], (NY, NX), ((0, 8),), -0.2, 0.2)), 0.5, 1.9)
    obs_cells = draw_obs_cells(jax.random.fold_in(streams_of[8], 71), 0)
    obs_fields = touch_ends(jax.random.randint(streams_of[3], (SUBWIN, OBS), 0, 3), jax.random.fold_in(streams_of[3], 1), 0, 2).astype(jnp.int32)
    obs_weight = jnp.clip(jnp.exp(math.log(0.5) - 2.3025851 * jax.random.uniform(streams_of[4], (SUBWIN, OBS), jnp.float32) ** level_of(streams_of[4], (SUBWIN, OBS), ((0, 4), (1, 8)), -0.2, 0.2)), 0.05, 0.5)
    innovation = bell_draw(streams_of[5], (SUBWIN, OBS), 1.0, 6.0, ((0, 4), (1, 8)), jnp.float32)
    transition = draw_transition(jax.random.fold_in(streams_of[8], 71), 0)
    model_error = jnp.clip(jnp.exp(jax.random.uniform(streams_of[7], (R,), jnp.float32, math.log(0.2), math.log(1.0))), 0.2, 1.0)
    return {"basis_fields": basis_fields, "mean_depth": mean_depth, "obs_cells": obs_cells, "obs_fields": obs_fields, "obs_weight": obs_weight, "innovation": innovation, "transition": transition, "model_error": model_error}


A_COEF = 0.5
B_COEF = 0.5
CORIOLIS = 0.3

def matmul_high(left, right):
    return jnp.dot(left, right, precision=lax.Precision.HIGHEST)

def diff_cols(values):
    return jnp.roll(values, -1, axis=-1) - jnp.roll(values, 1, axis=-1)

def diff_rows(values):
    padded = jnp.pad(values, ((0, 0), (1, 1), (0, 0)))
    return padded[:, 2:, :] - padded[:, :-2, :]

def advance(current, mean_depth):
    height, eastward, northward = (current[0], current[1], current[2])
    east_new = eastward + CORIOLIS * northward - A_COEF * diff_cols(height)
    north_new = northward - CORIOLIS * eastward - A_COEF * diff_rows(height)
    height_new = height - B_COEF * mean_depth * (diff_cols(east_new) + diff_rows(north_new))
    return jnp.stack([height_new, east_new, north_new])

def propagate(start_fields, mean_depth):
    current = start_fields.astype(jnp.float32)
    for repeat in range(STEPS):
        current = advance(current, mean_depth)
    return current

def unpack(packed):
    order = packed.shape[1]
    return (packed[:order], packed[order:2 * order], packed[2 * order:3 * order], packed[3 * order], packed[3 * order + 1])

def pack(trans, cov, prec, mean, info):
    return jnp.concatenate([trans, cov, prec, mean[None, :], info[None, :]], axis=0)

def inverse_of(matrix):
    return jnp.linalg.solve(matrix, jnp.eye(matrix.shape[0], dtype=jnp.float32))

def form_element(gram_sum, rhs_sum, transition, model_error, position):
    root_q = jnp.sqrt(model_error)
    coupled = transition * (position > 0).astype(jnp.float32)
    identity_mat = jnp.eye(gram_sum.shape[0], dtype=jnp.float32)
    system = identity_mat + root_q[:, None] * gram_sum * root_q[None, :]
    precise = inverse_of(system)
    trans = root_q[:, None] * matmul_high(precise, coupled / root_q[:, None])
    cov = root_q[:, None] * precise * root_q[None, :]
    vector = matmul_high(precise, root_q * rhs_sum)
    mean = root_q * vector
    info = matmul_high(coupled.T, vector / root_q)
    inner = matmul_high(precise, root_q[:, None] * gram_sum) / root_q[:, None]
    prec = matmul_high(coupled.T, matmul_high(inner, coupled))
    return pack(trans, cov, prec, mean, info)

def combine(earlier, latter):
    trans_one, cov_one, prec_one, mean_one, info_one = unpack(earlier)
    trans_two, cov_two, prec_two, mean_two, info_two = unpack(latter)
    identity_mat = jnp.eye(trans_one.shape[0], dtype=jnp.float32)
    system = identity_mat + matmul_high(cov_one, prec_two)
    inverse = inverse_of(system)
    scaled = matmul_high(trans_two, inverse)
    trans = matmul_high(scaled, trans_one)
    mean = matmul_high(scaled, mean_one + matmul_high(cov_one, info_two)) + mean_two
    cov = matmul_high(matmul_high(scaled, cov_one), trans_two.T) + cov_two
    back = inverse.T
    info = matmul_high(trans_one.T, matmul_high(back, info_two - matmul_high(prec_two, mean_one))) + info_one
    prec = matmul_high(trans_one.T, matmul_high(matmul_high(back, prec_two), trans_one)) + prec_one
    return pack(trans, cov, prec, mean, info)

def reference(basis_fields, mean_depth, obs_cells, obs_fields, obs_weight, innovation, transition, model_error):
    indices = jnp.arange(SUBWIN, dtype=jnp.int32)

    def one_window(index):
        current = propagate(basis_fields[index], mean_depth)
        flattened = current.reshape(3, R, NY * NX)
        projected = flattened[obs_fields[index], :, obs_cells[index]]
        weighted = projected * obs_weight[index][:, None]
        gram_sum = matmul_high(weighted.T, projected)
        rhs_sum = matmul_high(innovation[index] * obs_weight[index], projected)
        return form_element(gram_sum, rhs_sum, transition, model_error, index)
    elements = lax.map(one_window, indices)
    order = transition.shape[0]
    identity_pack = pack(jnp.eye(order, dtype=jnp.float32), jnp.zeros((order, order), jnp.float32), jnp.zeros((order, order), jnp.float32), jnp.zeros((order,), jnp.float32), jnp.zeros((order,), jnp.float32))

    def scan_turn(carry, element):
        joined = combine(carry, element)
        return (joined, joined[3 * order])
    unused, reduced_mean = lax.scan(scan_turn, identity_pack, elements)

    def rebuild(index):
        current = propagate(basis_fields[index], mean_depth)
        flattened = current.reshape(3, R, NY * NX)
        summed = jnp.einsum('r,frc->fc', reduced_mean[index], flattened, precision=lax.Precision.HIGHEST)
        return summed.reshape(3, NY, NX)
    increments = lax.map(rebuild, indices)
    return (reduced_mean, increments)
```

```python
import functools

import jax
import jax.numpy as jnp
from jax import lax
from jax.experimental import pallas as pl
from jax.experimental.pallas import tpu as pltpu
from jax.sharding import PartitionSpec as P

STEPS = 4
A_COEF = 0.5
B_COEF = 0.5
CORIOLIS = 0.3

F32 = jnp.float32
BF16 = jnp.bfloat16
LANES = 128
SUB = 8
REACH = 2 * STEPS
PADX = REACH + 1
FINE = 16
HIGH = lax.Precision.HIGHEST
NT = (((1,), (1,)), ((), ()))
NN = (((1,), (0,)), ((), ()))
TN = (((0,), (0,)), ((), ()))
VMEM = pl.BlockSpec(memory_space=pltpu.VMEM)
SMEM = pl.BlockSpec(memory_space=pltpu.SMEM)


def params(mib=60):
    return pltpu.CompilerParams(vmem_limit_bytes=mib << 20)


def dot6(left, right, dims=NN):
    return lax.dot_general(left, right, dims, precision=HIGH, preferred_element_type=F32)


def dot1(left, right, dims=NN):
    return lax.dot_general(left, right, dims, preferred_element_type=F32)


def halves(values):
    high = values.astype(BF16)
    return high, (values - high.astype(F32)).astype(BF16)


def thirds(values):
    high = values.astype(BF16)
    rest = values - high.astype(F32)
    mid = rest.astype(BF16)
    return high, mid, (rest - mid.astype(F32)).astype(BF16)


def dot3(left, right):
    (lh, ll), (rh, rl) = left, right
    return dot1(lh, rh) + (dot1(lh, rl) + dot1(ll, rh))


def window_rows(own_slot, rows, scal_ref, own_ref, first_ref, second_ref, obs_ref):
    even = scal_ref[0] == 0
    own = own_ref[0:rows, :] * B_COEF
    first = first_ref[0:rows, :] * B_COEF
    if own_slot:
        second = second_ref[0:rows, :] * B_COEF
        above = jnp.where(even, second, first)
        below = jnp.where(even, first, second)
        domain = jnp.concatenate([above[rows // 2 :], own, below[: rows // 2]], axis=0)
        base = rows // 2
    else:
        domain = jnp.concatenate(
            [jnp.where(even, own, first), jnp.where(even, first, own)], axis=0
        )
        base = jnp.where(even, rows, 0)
    return domain, base


def project_kernel(
    own_slot, rows, nx, scal_ref, own_ref, first_ref, second_ref, basis_ref, out_ref,
    bmw, p, g, qp, sp, w, sh, sl,
):
    obs_ref = own_ref if own_slot else first_ref
    domain, base = window_rows(
        own_slot, rows, scal_ref, own_ref, first_ref, second_ref, obs_ref
    )
    depth = 2 * rows
    nob = obs_ref.shape[1] // LANES
    inner = REACH - 2
    rolled = [
        pltpu.roll(domain, (-dx) % nx, 1) if dx else domain for dx in range(-inner, inner + 1)
    ]
    stacked = jnp.concatenate(rolled, axis=0)
    pieces = thirds(stacked)
    cells = obs_ref[rows : rows + 1, :]
    fields = obs_ref[rows + 1 : rows + 2, :]
    row_all = jnp.floor(cells * (1.0 / nx))
    col = (cells - row_all * nx).astype(jnp.int32)
    row = (row_all - rows * jnp.floor(row_all * (1.0 / rows))).astype(jnp.int32) + base
    field = fields.astype(jnp.int32)
    y_iota = lax.broadcasted_iota(jnp.int32, (depth, LANES), 0)
    x_iota = lax.broadcasted_iota(jnp.int32, (nx, LANES), 0)
    if own_slot:
        first_row = jnp.where(scal_ref[1] == 0, rows // 2, 0)
        last_row = jnp.where(scal_ref[1] == scal_ref[2] - 1, rows // 2 + rows, depth)
        inside = ((y_iota >= first_row) & (y_iota < last_row)).astype(F32)
    lo, hi = SUB, SUB + depth
    zero_rows = jnp.zeros((SUB, LANES), F32)
    for ob in range(nob):
        lane = slice(ob * LANES, (ob + 1) * LANES)
        onehot = (x_iota == col[:, lane]).astype(F32).astype(BF16)
        depths = dot1(pieces[0], onehot) + (dot1(pieces[1], onehot) + dot1(pieces[2], onehot))
        for i in range(2 * inner + 1):
            bmw[ob, i] = depths[i * depth : (i + 1) * depth]
        for i in range(2 * PADX + 1):
            g[ob, i, 0:lo] = zero_rows
            g[ob, i, hi : hi + SUB] = zero_rows
            sp[ob, i, 0:lo] = zero_rows
            sp[ob, i, hi : hi + SUB] = zero_rows
        at_row = y_iota == row[:, lane]
        start = [(at_row & (field[:, lane] == f)).astype(F32) for f in range(3)]

        def at(ref, dx):
            return ref[ob, dx + PADX, lo:hi]

        def slope(ref, dx):
            return ref[ob, dx + PADX, lo + 1 : hi + 1] - ref[ob, dx + PADX, lo - 1 : hi - 1]

        p[ob, PADX, lo:hi] = start[0]
        for step in range(STEPS):
            reach = 2 * step
            for dx in range(-reach, reach + 1):
                g[ob, dx + PADX, lo:hi] = bmw[ob, dx + inner] * at(p, dx)
            for dx in range(-reach - 1, reach + 2):
                if step == 0:
                    east, north = (start[1], start[2]) if dx == 0 else (None, None)
                elif abs(dx) <= reach - 2:
                    qv, sv = at(qp, dx), at(sp, dx)
                    east, north = qv - CORIOLIS * sv, sv + CORIOLIS * qv
                elif abs(dx) == reach - 1:
                    east = at(qp, dx)
                    north = CORIOLIS * east
                else:
                    east, north = None, None
                if abs(dx + 1) <= reach:
                    east = at(g, dx + 1) if east is None else east + at(g, dx + 1)
                if abs(dx - 1) <= reach:
                    east = -at(g, dx - 1) if east is None else east - at(g, dx - 1)
                qp[ob, dx + PADX, lo:hi] = east
                if abs(dx) <= reach:
                    rise = slope(g, dx)
                    north = rise if north is None else north + rise
                    if own_slot:
                        north = north * inside
                    sp[ob, dx + PADX, lo:hi] = north
            for dx in range(-reach - 2, reach + 3):
                change = None
                if abs(dx + 1) <= reach + 1:
                    change = at(qp, dx + 1)
                if abs(dx - 1) <= reach + 1:
                    change = -at(qp, dx - 1) if change is None else change - at(qp, dx - 1)
                if abs(dx) <= reach:
                    change = change + slope(sp, dx)
                change = A_COEF * change
                if abs(dx) <= reach:
                    change = change + at(p, dx)
                p[ob, dx + PADX, lo:hi] = change

        if own_slot:
            picked = slice(lo + rows // 2, lo + rows // 2 + rows)
        else:
            picked = pl.ds(pl.multiple_of(jnp.where(even_of(scal_ref), lo, lo + rows), SUB), rows)
        shift = lax.rem(col[:, lane] + (nx - REACH), nx)
        fine = jnp.broadcast_to(lax.rem(shift, FINE), (rows, LANES))
        bits = [(fine & (1 << i)) != 0 for i in range(4)]
        coarse = jnp.broadcast_to(shift // FINE, (FINE, LANES))
        blocks = nx // FINE
        marks = [(coarse == block).astype(F32).astype(BF16) for block in range(blocks)]
        zero = jnp.zeros((rows, LANES), F32)
        for f in range(3):
            values = [None] * (2 * FINE)
            for dx in range(-REACH, REACH + 1):
                if f == 0:
                    value = p[ob, dx + PADX, picked]
                elif abs(dx) <= REACH - 2:
                    qv, sv = qp[ob, dx + PADX, picked], sp[ob, dx + PADX, picked]
                    value = qv - CORIOLIS * sv if f == 1 else sv + CORIOLIS * qv
                elif abs(dx) == REACH - 1:
                    qv = qp[ob, dx + PADX, picked]
                    value = qv if f == 1 else CORIOLIS * qv
                else:
                    value = None
                values[dx + REACH] = value
            for i in range(4):
                moved = []
                for e in range(2 * FINE):
                    here = values[e]
                    there = values[e - (1 << i)] if e >= (1 << i) else None
                    if here is None and there is None:
                        moved.append(None)
                    else:
                        moved.append(
                            jnp.where(
                                bits[i],
                                zero if there is None else there,
                                zero if here is None else here,
                            )
                        )
                values = moved
            for e in range(2 * FINE):
                w[e * rows : (e + 1) * rows, :] = zero if values[e] is None else values[e]
            for y in range(rows):
                both = halves(w[pl.ds(y, 2 * FINE, stride=rows), :])
                for part, ref in zip(both, (sh, sl)):
                    near, far = part[:FINE], part[FINE:]
                    for block in range(blocks):
                        start_row = (f * rows + y) * nx + block * FINE
                        ref[start_row : start_row + FINE, lane] = (
                            near * marks[block] + far * marks[block - 1]
                        )
    out_ref[...] = dot1(basis_ref[...], sh[...]) + dot1(basis_ref[...], sl[...])


def even_of(scal_ref):
    return scal_ref[0] == 0


def project(own_slot, scal, own, first, second, basis, rows, nx):
    order, depth_all = basis.shape
    nobs = own.shape[1]
    nob = nobs // LANES
    wide = (nob, 2 * PADX + 1, 2 * rows + 2 * SUB, LANES)
    return pl.pallas_call(
        functools.partial(project_kernel, own_slot, rows, nx),
        out_shape=jax.ShapeDtypeStruct((order, nobs), F32),
        in_specs=[SMEM] + [VMEM] * 4,
        out_specs=VMEM,
        scratch_shapes=[
            pltpu.VMEM((nob, 2 * REACH - 3, 2 * rows, LANES), F32),
            pltpu.VMEM(wide, F32),
            pltpu.VMEM(wide, F32),
            pltpu.VMEM(wide, F32),
            pltpu.VMEM(wide, F32),
            pltpu.VMEM((2 * FINE * rows, LANES), F32),
            pltpu.VMEM((depth_all, nobs), BF16),
            pltpu.VMEM((depth_all, nobs), BF16),
        ],
        compiler_params=params(48),
        cost_estimate=pl.CostEstimate(
            flops=4 * order * depth_all * nobs,
            bytes_accessed=2 * order * depth_all,
            transcendentals=0,
        ),
        name="project_own" if own_slot else "project_partner",
    )(scal, own, first, second, basis)


def triangle_masks(half):
    rows = lax.broadcasted_iota(jnp.int32, (half, half), 0)
    cols = lax.broadcasted_iota(jnp.int32, (half, half), 1)
    return rows, cols


def store_packed(out_ref, matrix, vector):
    half = matrix.shape[0] // 2
    rows, cols = triangle_masks(half)
    corner = matrix[half:, half:]
    out_ref[0:half] = jnp.where(rows >= cols, matrix[:half, :half], corner)
    out_ref[half : 2 * half] = matrix[half:, :half]
    diagonal = jnp.sum(jnp.where(rows == cols, corner, 0.0), axis=0, keepdims=True)
    tail = jnp.concatenate(
        [vector[:, :half], vector[:, half:], diagonal, jnp.zeros((SUB - 3, half), F32)], axis=0
    )
    out_ref[2 * half : 2 * half + SUB] = tail


def load_packed(values):
    half = values.shape[1]
    rows, cols = triangle_masks(half)
    mixed = values[0:half]
    cross = values[half : 2 * half]
    vector = jnp.concatenate(
        [values[2 * half : 2 * half + 1], values[2 * half + 1 : 2 * half + 2]], axis=1
    )
    diagonal = values[2 * half + 2 : 2 * half + 3]
    turned = mixed.T
    first = jnp.where(rows >= cols, mixed, turned)
    last = jnp.where(rows == cols, diagonal, jnp.where(rows < cols, mixed, turned))
    top = jnp.concatenate([first, cross.T], axis=1)
    bottom = jnp.concatenate([cross, last], axis=1)
    return jnp.concatenate([top, bottom], axis=0), vector


def gram_kernel(own_ref, first_ref, second_ref, weight_ref, innovation_ref, out_ref):
    projected = own_ref[...] + first_ref[...] + second_ref[...]
    weight = weight_ref[...]
    gram = dot6(projected * weight, projected, NT)
    pulled = jnp.broadcast_to(weight * innovation_ref[...], (SUB, weight.shape[1]))
    rhs = dot6(pulled, projected, NT)[0:1]
    store_packed(out_ref, gram, rhs)


def gram(own, first, second, weight, innovation):
    order = own.shape[0]
    return pl.pallas_call(
        gram_kernel,
        out_shape=jax.ShapeDtypeStruct((order + SUB, order // 2), F32),
        in_specs=[VMEM] * 5,
        out_specs=VMEM,
        compiler_params=params(),
        name="gram",
    )(own, first, second, weight, innovation)


def identity_like(matrix):
    rows = lax.broadcasted_iota(jnp.int32, matrix.shape, 0)
    cols = lax.broadcasted_iota(jnp.int32, matrix.shape, 1)
    return (rows == cols).astype(F32)


def norm_of(matrix):
    size = jnp.abs(matrix)
    return jnp.minimum(jnp.max(jnp.sum(size, axis=0)), jnp.max(jnp.sum(size, axis=1)))


def invert_shifted(offdiags, refine, tol):
    eye = identity_like(offdiags[0])
    systems = [halves(eye + m) for m in offdiags]
    starts, errors = [], []
    for m in offdiags:
        bound = norm_of(m)
        alpha = 2.0 / (2.0 + bound)
        error = bound / (2.0 + bound)
        scale = 2.0 / (2.0 - error * error)
        starts.append((scale * alpha) * (2.0 * eye - alpha * (eye + m)))
        errors.append(error * error / (2.0 - error * error))

    def unfinished(state):
        return functools.reduce(jnp.maximum, state[1]) > tol

    def turn(state):
        estimates, errors = state
        new_estimates, new_errors = [], []
        for system, estimate, error in zip(systems, estimates, errors):
            parts = halves(estimate)
            residual = 2.0 * eye - dot3(system, parts)
            scale = 2.0 / (2.0 - error * error)
            new_estimates.append(scale * dot3(parts, halves(residual)))
            new_errors.append(error * error / (2.0 - error * error))
        return tuple(new_estimates), tuple(new_errors)

    estimates, errors = lax.while_loop(unfinished, turn, (tuple(starts), tuple(errors)))
    if not refine:
        return estimates
    bound = functools.reduce(jnp.maximum, [norm_of(m) for m in offdiags])
    turns = jnp.where(bound > 300.0, 4, 1)

    def polish(index, estimates):
        result = []
        for m, estimate in zip(offdiags, estimates):
            residual = eye - estimate - dot6(m, estimate)
            result.append(estimate + dot3(halves(estimate), halves(residual)))
        return tuple(result)

    return lax.fori_loop(0, turns, polish, estimates)


def times(matrix, row):
    return dot6(jnp.broadcast_to(row, (SUB, row.shape[1])), matrix, NT)[0:1]


def times_left(matrix, row):
    return dot6(jnp.broadcast_to(row, (SUB, row.shape[1])), matrix, NN)[0:1]


def column(row):
    size = row.shape[1]
    return jnp.broadcast_to(row, (size, size)).T


def pair_kernel(
    full, scal_ref, mine_ref, other_ref, transition_ref, model_error_ref,
    a_ref, j_ref, vec_ref, prefix_ref, *more,
):
    lower_core = scal_ref[0] == 0
    first_pair = scal_ref[1] == 0
    mine, other = mine_ref[...], other_ref[...]
    q2 = model_error_ref[...]
    root_row = jnp.sqrt(q2)
    root_col = column(root_row)
    q2_col = column(q2)
    transition = transition_ref[...]
    moves = [jnp.where(first_pair, 0.0, transition), transition]
    grams, rhss = [], []
    for packed in (jnp.where(lower_core, mine, other), jnp.where(lower_core, other, mine)):
        matrix, vector = load_packed(packed)
        grams.append(matrix)
        rhss.append(vector)
    precise = invert_shifted([root_col * m * root_row for m in grams], True, 2e-3)
    elements = []
    for inverse, rhs, move in zip(precise, rhss, moves):
        cov = root_col * inverse * root_row
        mean = times(cov, rhs)
        scaled = move / q2_col
        trans = dot6(cov, scaled)
        prec = dot6(scaled, move - trans, TN)
        info = times_left(scaled, mean)
        elements.append((trans, mean, cov, info, prec))
    (a1, b1, c1, eta1, j1), (a2, b2, c2, eta2, j2) = elements
    (inverse,) = invert_shifted([dot6(c1, j2)], True, 1e-3)
    outer = dot6(c1, a2, NT)
    spread = dot6(j2, a1)
    ahead = b1 + times(c1, eta2)
    behind = eta2 - times(j2, b1)
    scaled = dot6(a2, inverse)
    back = dot6(inverse, a1)
    cov = dot6(scaled, outer) + c2
    trans = dot6(scaled, a1)
    prec = dot6(back, spread, TN) + j1
    mean = times(scaled, ahead) + b2
    info = times_left(back, behind) + eta1
    a_ref[...] = jnp.where(lower_core, a1, trans)
    j_ref[...] = jnp.where(lower_core, j1, prec)
    vec_ref[0:1] = jnp.where(lower_core, b1, mean)
    vec_ref[1:2] = jnp.where(lower_core, eta1, info)
    vec_ref[2:3] = mean
    vec_ref[3:4] = info
    vec_ref[4:SUB] = jnp.zeros((SUB - 4, mean.shape[1]), F32)
    store_packed(prefix_ref, cov, mean)
    if full:
        for ref, value in zip(more, (trans, prec, cov)):
            ref[...] = value


def pair_up(scal, mine, other, transition, model_error, full):
    order = transition.shape[0]
    square = jax.ShapeDtypeStruct((order, order), F32)
    shapes = [
        square,
        square,
        jax.ShapeDtypeStruct((SUB, order), F32),
        jax.ShapeDtypeStruct(mine.shape, F32),
    ] + [square] * (3 if full else 0)
    return pl.pallas_call(
        functools.partial(pair_kernel, full),
        out_shape=shapes,
        in_specs=[SMEM] + [VMEM] * 4,
        out_specs=[VMEM] * len(shapes),
        compiler_params=params(),
        name="pair_up",
    )(scal, mine, other, transition, model_error)


def advance_kernel(incoming_ref, a_ref, j_ref, c_ref, vec_ref, out_ref):
    cov0, mean0 = load_packed(incoming_ref[...])
    (inverse,) = invert_shifted([dot6(cov0, j_ref[...])], True, 1e-3)
    scaled = dot6(a_ref[...], inverse)
    mean = times(scaled, mean0 + times(cov0, vec_ref[3:4])) + vec_ref[2:3]
    cov = dot6(scaled, dot6(cov0, a_ref[...], NT)) + c_ref[...]
    store_packed(out_ref, cov, mean)


def advance_prefix(incoming, a, j, c, vec):
    return pl.pallas_call(
        advance_kernel,
        out_shape=jax.ShapeDtypeStruct(incoming.shape, F32),
        in_specs=[VMEM] * 5,
        out_specs=VMEM,
        compiler_params=params(),
        name="advance_prefix",
    )(incoming, a, j, c, vec)


def finish_kernel(rows, nx, incoming_ref, a_ref, j_ref, vec_ref, basis_ref, mean_ref, sum_ref):
    cov0, mean0 = load_packed(incoming_ref[...])
    start = mean0 + times(cov0, vec_ref[1:2])
    middle = dot6(cov0, j_ref[...])
    (inverse,) = invert_shifted([middle], True, 1e-3)
    guess = times(inverse, start)
    guess = guess + times(inverse, start - guess - times(middle, guess))
    mean = times(a_ref[...], guess) + vec_ref[0:1]
    mean_ref[...] = mean
    pieces = jnp.concatenate(list(thirds(mean)) + [jnp.zeros((5, mean.shape[1]), BF16)], axis=0)
    sums = dot1(pieces, basis_ref[...])
    total = sums[0:1] + (sums[1:2] + sums[2:3])
    for i in range(3 * rows):
        sum_ref[i : i + 1, :] = total[:, i * nx : (i + 1) * nx]


def finish(incoming, a, j, vec, basis, rows, nx):
    order = a.shape[0]
    return pl.pallas_call(
        functools.partial(finish_kernel, rows, nx),
        out_shape=[
            jax.ShapeDtypeStruct((1, order), F32),
            jax.ShapeDtypeStruct((3 * rows, nx), F32),
        ],
        in_specs=[VMEM] * 5,
        out_specs=[VMEM] * 2,
        compiler_params=params(),
        name="finish",
    )(incoming, a, j, vec, basis)


def increments_kernel(rows, nx, scal_ref, own_ref, first_ref, second_ref, mo, mf, ms, out_ref):
    even = even_of(scal_ref)

    def extend(own, first, second):
        above = jnp.where(even, second, first)
        below = jnp.where(even, first, second)
        return jnp.concatenate([above, own, below], axis=0)

    depth = extend(mo[0:rows, :], mf[0:rows, :], ms[0:rows, :]) * B_COEF
    h, u, v = [
        extend(*(ref[f * rows : (f + 1) * rows, :] for ref in (own_ref, first_ref, second_ref)))
        for f in range(3)
    ]
    total = 3 * rows
    y_iota = lax.broadcasted_iota(jnp.int32, (total, nx), 0)
    first_row = jnp.where(scal_ref[1] == 0, rows, 0)
    last_row = jnp.where(scal_ref[1] == scal_ref[2] - 1, 2 * rows, total)
    inside = ((y_iota >= first_row) & (y_iota < last_row)).astype(F32)

    def diff_cols(values):
        return pltpu.roll(values, nx - 1, 1) - pltpu.roll(values, 1, 1)

    def diff_rows(values):
        return pltpu.roll(values, total - 1, 0) - pltpu.roll(values, 1, 0)

    for step in range(STEPS):
        east = u + CORIOLIS * v - A_COEF * diff_cols(h)
        north = (v - CORIOLIS * u - A_COEF * diff_rows(h)) * inside
        h = h - depth * (diff_cols(east) + diff_rows(north))
        u, v = east, north
    for f, values in enumerate((h, u, v)):
        out_ref[f] = values[rows : 2 * rows]


def propagate_sum(scal, own, first, second, mo, mf, ms, rows, nx):
    return pl.pallas_call(
        functools.partial(increments_kernel, rows, nx),
        out_shape=jax.ShapeDtypeStruct((3, rows, nx), F32),
        in_specs=[SMEM] + [VMEM] * 6,
        out_specs=VMEM,
        compiler_params=params(),
        name="propagate_sum",
    )(scal, own, first, second, mo, mf, ms)


def on_device(
    basis_fields, mean_depth, obs_cells, obs_fields, obs_weight, innovation, transition, model_error
):
    order, rows, nx = basis_fields.shape[2:]
    tiles = lax.axis_size("tile")
    windows = lax.axis_size("tm")
    tile = lax.axis_index("tile")
    window = lax.axis_index("tm")
    near = [(i, i ^ 1) for i in range(tiles)]
    far = [(i, i + 1) for i in range(1, tiles - 1, 2)]
    far = far + [(b, a) for a, b in far]
    scal = jnp.stack([tile % 2, tile, jnp.int32(tiles)]).astype(jnp.int32)
    scal_far = jnp.stack([1 - tile % 2, tile, jnp.int32(tiles)]).astype(jnp.int32)

    info = jnp.concatenate(
        [
            mean_depth,
            obs_cells.astype(F32),
            obs_fields.astype(F32),
            jnp.zeros((SUB - 2, nx), F32),
        ],
        axis=0,
    )
    info_near = lax.ppermute(info, "tile", near)
    info_far = lax.ppermute(info, "tile", far)
    basis = basis_fields[0].transpose(1, 0, 2, 3).reshape(order, 3 * rows * nx)

    part_near = project(False, scal, info, info_near, info_near, basis, rows, nx)
    got_near = lax.ppermute(part_near, "tile", near)
    part_far = project(False, scal_far, info, info_far, info_far, basis, rows, nx)
    got_far = lax.ppermute(part_far, "tile", far)
    part_own = project(True, scal, info, info_near, info_far, basis, rows, nx)

    packed = gram(part_own, got_near, got_far, obs_weight, innovation)
    bit = 1
    while bit < tiles:
        packed = packed + lax.ppermute(packed, "tile", [(i, i ^ bit) for i in range(tiles)])
        bit *= 2

    other = lax.ppermute(packed, "tm", [(i, i ^ 1) for i in range(windows)])
    pairs = windows // 2
    scal_tm = jnp.stack([window % 2, window // 2]).astype(jnp.int32)
    a, j, vec, prefix, *more = pair_up(
        scal_tm, packed, other, transition, model_error[None, :], pairs > 2
    )
    incoming = jnp.zeros_like(prefix)
    for turn in range(pairs - 1):
        incoming = lax.ppermute(prefix, "tm", [(i, i + 2) for i in range(windows - 2)])
        if turn < pairs - 2:
            longer = advance_prefix(incoming, *more, vec)
            prefix = jnp.where(window // 2 == turn + 1, longer, prefix)
    mean, sums = finish(incoming, a, j, vec, basis, rows, nx)
    sums_near = lax.ppermute(sums, "tile", near)
    sums_far = lax.ppermute(sums, "tile", far)
    result = propagate_sum(
        scal, sums, sums_near, sums_far, info, info_near, info_far, rows, nx
    )
    return mean, result[None]


def solution(mesh):
    return jax.shard_map(
        on_device,
        mesh=mesh,
        in_specs=(
            P("tm", None, None, "tile", None),
            P("tile", None),
            P("tm", "tile"),
            P("tm", "tile"),
            P("tm", "tile"),
            P("tm", "tile"),
            P(),
            P(),
        ),
        out_specs=(P("tm", None), P("tm", None, "tile", None)),
        check_vma=False,
    )
```

```python
import functools

import jax
import jax.numpy as jnp
from jax import lax
from jax.experimental import pallas as pl
from jax.experimental.pallas import tpu as pltpu
from jax.sharding import PartitionSpec as P

STEPS = 4
A_COEF = 0.5
B_COEF = 0.5
CORIOLIS = 0.3

F32 = jnp.float32
BF16 = jnp.bfloat16
LANES = 128
SUB = 8
REACH = 2 * STEPS
PADX = REACH + 1
NEAR, FAR, OWN = "project_near", "project_far", "project_own"
FINE = 16
HIGH = lax.Precision.HIGHEST
NT = (((1,), (1,)), ((), ()))
NN = (((1,), (0,)), ((), ()))
TN = (((0,), (0,)), ((), ()))
VMEM = pl.BlockSpec(memory_space=pltpu.VMEM)


def params(mib):
    return pltpu.CompilerParams(vmem_limit_bytes=mib << 20)


def dot6(left, right, dims=NN):
    return lax.dot_general(left, right, dims, precision=HIGH, preferred_element_type=F32)


def dot1(left, right, dims=NN):
    return lax.dot_general(left, right, dims, preferred_element_type=F32)


def halves(values):
    high = values.astype(BF16)
    return high, (values - high.astype(F32)).astype(BF16)


def thirds(values):
    high = values.astype(BF16)
    rest = values - high.astype(F32)
    mid = rest.astype(BF16)
    return high, mid, (rest - mid.astype(F32)).astype(BF16)


def dot3(left, right, dims=NN):
    (lh, ll), (rh, rl) = left, right
    return dot1(lh, rh, dims) + (dot1(lh, rl, dims) + dot1(ll, rh, dims))


def before_after(first, second):
    tile, tiles = lax.axis_index("tile"), lax.axis_size("tile")
    even = lax.rem(tile, 2) == 0
    before = jnp.where(even, jnp.where(tile == 0, 0.0, second), first)
    after = jnp.where(even, first, jnp.where(tile == tiles - 1, 0.0, second))
    return before, after


def window_rows(slot, rows, even, own_ref, first_ref, second_ref):
    own = own_ref[0:rows, :] * B_COEF
    first = first_ref[0:rows, :] * B_COEF
    if slot == OWN:
        second = second_ref[0:rows, :] * B_COEF
        above, below = before_after(first, second)
        domain = jnp.concatenate([above[rows // 2 :], own, below[: rows // 2]], axis=0)
        base = rows // 2
    else:
        domain = jnp.concatenate(
            [jnp.where(even, own, first), jnp.where(even, first, own)], axis=0
        )
        base = jnp.where(even, rows, 0)
    return domain, base


def project_kernel(
    slot, rows, nx, own_ref, first_ref, second_ref, basis_ref, out_ref,
    bmw, p, g, qp, sp, w, sh, sl,
):
    own_slot = slot == OWN
    obs_ref = own_ref if own_slot else first_ref
    tile, tiles = lax.axis_index("tile"), lax.axis_size("tile")
    even = lax.rem(tile, 2) == (1 if slot == FAR else 0)
    domain, base = window_rows(slot, rows, even, own_ref, first_ref, second_ref)
    depth = 2 * rows
    nob = obs_ref.shape[1] // LANES
    inner = REACH - 2
    rolled = [
        pltpu.roll(domain, (-dx) % nx, 1) if dx else domain for dx in range(-inner, inner + 1)
    ]
    stacked = jnp.concatenate(rolled, axis=0)
    pieces = thirds(stacked)
    cells = obs_ref[rows : rows + 1, :]
    fields = obs_ref[rows + 1 : rows + 2, :]
    row_all = jnp.floor(cells * (1.0 / nx))
    col = (cells - row_all * nx).astype(jnp.int32)
    row = (row_all - rows * jnp.floor(row_all * (1.0 / rows))).astype(jnp.int32) + base
    field = fields.astype(jnp.int32)
    y_iota = lax.broadcasted_iota(jnp.int32, (depth, LANES), 0)
    x_iota = lax.broadcasted_iota(jnp.int32, (nx, LANES), 0)
    if own_slot:
        first_row = jnp.where(tile == 0, rows // 2, 0)
        last_row = jnp.where(tile == tiles - 1, rows // 2 + rows, depth)
        inside = ((y_iota >= first_row) & (y_iota < last_row)).astype(F32)
    lo, hi = SUB, SUB + depth
    zero_rows = jnp.zeros((SUB, LANES), F32)
    for ob in range(nob):
        lane = slice(ob * LANES, (ob + 1) * LANES)
        onehot = (x_iota == col[:, lane]).astype(F32).astype(BF16)
        depths = dot1(pieces[0], onehot) + (dot1(pieces[1], onehot) + dot1(pieces[2], onehot))
        for i in range(2 * inner + 1):
            bmw[ob, i] = depths[i * depth : (i + 1) * depth]
        for i in range(2 * PADX + 1):
            g[ob, i, 0:lo] = zero_rows
            g[ob, i, hi : hi + SUB] = zero_rows
            sp[ob, i, 0:lo] = zero_rows
            sp[ob, i, hi : hi + SUB] = zero_rows
        at_row = y_iota == row[:, lane]
        start = [(at_row & (field[:, lane] == f)).astype(F32) for f in range(3)]

        def at(ref, dx):
            return ref[ob, dx + PADX, lo:hi]

        def slope(ref, dx):
            return ref[ob, dx + PADX, lo + 1 : hi + 1] - ref[ob, dx + PADX, lo - 1 : hi - 1]

        p[ob, PADX, lo:hi] = start[0]
        for step in range(STEPS):
            reach = 2 * step
            for dx in range(-reach, reach + 1):
                g[ob, dx + PADX, lo:hi] = bmw[ob, dx + inner] * at(p, dx)
            for dx in range(-reach - 1, reach + 2):
                if step == 0:
                    east, north = (start[1], start[2]) if dx == 0 else (None, None)
                elif abs(dx) <= reach - 2:
                    qv, sv = at(qp, dx), at(sp, dx)
                    east, north = qv - CORIOLIS * sv, sv + CORIOLIS * qv
                elif abs(dx) == reach - 1:
                    east = at(qp, dx)
                    north = CORIOLIS * east
                else:
                    east, north = None, None
                if abs(dx + 1) <= reach:
                    east = at(g, dx + 1) if east is None else east + at(g, dx + 1)
                if abs(dx - 1) <= reach:
                    east = -at(g, dx - 1) if east is None else east - at(g, dx - 1)
                qp[ob, dx + PADX, lo:hi] = east
                if abs(dx) <= reach:
                    rise = slope(g, dx)
                    north = rise if north is None else north + rise
                    if own_slot:
                        north = north * inside
                    sp[ob, dx + PADX, lo:hi] = north
            for dx in range(-reach - 2, reach + 3):
                change = None
                if abs(dx + 1) <= reach + 1:
                    change = at(qp, dx + 1)
                if abs(dx - 1) <= reach + 1:
                    change = -at(qp, dx - 1) if change is None else change - at(qp, dx - 1)
                if abs(dx) <= reach:
                    change = change + slope(sp, dx)
                change = A_COEF * change
                if abs(dx) <= reach:
                    change = change + at(p, dx)
                p[ob, dx + PADX, lo:hi] = change

        if own_slot:
            picked = slice(lo + rows // 2, lo + rows // 2 + rows)
        else:
            picked = pl.ds(pl.multiple_of(jnp.where(even, lo, lo + rows), SUB), rows)
        shift = lax.rem(col[:, lane] + (nx - REACH), nx)
        fine = jnp.broadcast_to(lax.rem(shift, FINE), (rows, LANES))
        bits = [(fine & (1 << i)) != 0 for i in range(4)]
        coarse = jnp.broadcast_to(shift // FINE, (FINE, LANES))
        blocks = nx // FINE
        marks = [(coarse == block).astype(F32).astype(BF16) for block in range(blocks)]
        zero = jnp.zeros((rows, LANES), F32)
        for f in range(3):
            values = [None] * (2 * FINE)
            for dx in range(-REACH, REACH + 1):
                if f == 0:
                    value = p[ob, dx + PADX, picked]
                elif abs(dx) <= REACH - 2:
                    qv, sv = qp[ob, dx + PADX, picked], sp[ob, dx + PADX, picked]
                    value = qv - CORIOLIS * sv if f == 1 else sv + CORIOLIS * qv
                elif abs(dx) == REACH - 1:
                    qv = qp[ob, dx + PADX, picked]
                    value = qv if f == 1 else CORIOLIS * qv
                else:
                    value = None
                values[dx + REACH] = value
            for i in range(4):
                moved = []
                for e in range(2 * FINE):
                    here = values[e]
                    there = values[e - (1 << i)] if e >= (1 << i) else None
                    if here is None and there is None:
                        moved.append(None)
                    else:
                        moved.append(
                            jnp.where(
                                bits[i],
                                zero if there is None else there,
                                zero if here is None else here,
                            )
                        )
                values = moved
            for e in range(2 * FINE):
                w[e * rows : (e + 1) * rows, :] = zero if values[e] is None else values[e]
            for y in range(rows):
                both = halves(w[pl.ds(y, 2 * FINE, stride=rows), :])
                for part, ref in zip(both, (sh, sl)):
                    near, far = part[:FINE], part[FINE:]
                    for block in range(blocks):
                        start_row = (f * rows + y) * nx + block * FINE
                        ref[start_row : start_row + FINE, lane] = (
                            near * marks[block] + far * marks[block - 1]
                        )
    out_ref[...] = dot1(basis_ref[...], sh[...]) + dot1(basis_ref[...], sl[...])


def project(slot, own, first, second, basis, rows, nx):
    order, depth_all = basis.shape
    nobs = own.shape[1]
    nob = nobs // LANES
    wide = (nob, 2 * PADX + 1, 2 * rows + 2 * SUB, LANES)
    return pl.pallas_call(
        functools.partial(project_kernel, slot, rows, nx),
        out_shape=jax.ShapeDtypeStruct((order, nobs), F32),
        in_specs=[VMEM] * 4,
        out_specs=VMEM,
        scratch_shapes=[
            pltpu.VMEM((nob, 2 * REACH - 3, 2 * rows, LANES), F32),
            pltpu.VMEM(wide, F32),
            pltpu.VMEM(wide, F32),
            pltpu.VMEM(wide, F32),
            pltpu.VMEM(wide, F32),
            pltpu.VMEM((2 * FINE * rows, LANES), F32),
            pltpu.VMEM((depth_all, nobs), BF16),
            pltpu.VMEM((depth_all, nobs), BF16),
        ],
        compiler_params=params(48),
        cost_estimate=pl.CostEstimate(
            flops=4 * order * depth_all * nobs,
            bytes_accessed=2 * order * depth_all,
            transcendentals=0,
        ),
        name=slot,
    )(own, first, second, basis)


def triangle_masks(half):
    rows = lax.broadcasted_iota(jnp.int32, (half, half), 0)
    cols = lax.broadcasted_iota(jnp.int32, (half, half), 1)
    return rows, cols


def store_packed(out_ref, matrix, vector):
    half = matrix.shape[0] // 2
    rows, cols = triangle_masks(half)
    corner = matrix[half:, half:]
    out_ref[0:half] = jnp.where(rows >= cols, matrix[:half, :half], corner)
    out_ref[half : 2 * half] = matrix[half:, :half]
    diagonal = jnp.sum(jnp.where(rows == cols, corner, 0.0), axis=0, keepdims=True)
    tail = jnp.concatenate(
        [vector[:, :half], vector[:, half:], diagonal, jnp.zeros((SUB - 3, half), F32)], axis=0
    )
    out_ref[2 * half : 2 * half + SUB] = tail


def load_packed(values):
    half = values.shape[1]
    rows, cols = triangle_masks(half)
    mixed = values[0:half]
    cross = values[half : 2 * half]
    vector = jnp.concatenate(
        [values[2 * half : 2 * half + 1], values[2 * half + 1 : 2 * half + 2]], axis=1
    )
    diagonal = values[2 * half + 2 : 2 * half + 3]
    turned = mixed.T
    first = jnp.where(rows >= cols, mixed, turned)
    last = jnp.where(rows == cols, diagonal, jnp.where(rows < cols, mixed, turned))
    top = jnp.concatenate([first, cross.T], axis=1)
    bottom = jnp.concatenate([cross, last], axis=1)
    return jnp.concatenate([top, bottom], axis=0), vector


def with_row(matrix, row):
    return jnp.concatenate([matrix, jnp.broadcast_to(row, (SUB, row.shape[1]))], axis=0)


def gram_kernel(own_ref, first_ref, second_ref, weight_ref, innovation_ref, out_ref):
    tile, tiles = lax.axis_index("tile"), lax.axis_size("tile")
    inner = (tile != 0) & (tile != tiles - 1)
    projected = own_ref[...] + first_ref[...] + jnp.where(inner, second_ref[...], 0.0)
    weight = weight_ref[...]
    left = with_row(projected * weight, weight * innovation_ref[...])
    result = dot3(halves(left), halves(projected), NT)
    size = projected.shape[0]
    store_packed(out_ref, result[:size], result[size : size + 1])


def gram(own, first, second, weight, innovation):
    order = own.shape[0]
    return pl.pallas_call(
        gram_kernel,
        out_shape=jax.ShapeDtypeStruct((order + SUB, order // 2), F32),
        in_specs=[VMEM] * 5,
        out_specs=VMEM,
        compiler_params=params(8),
        name="gram",
    )(own, first, second, weight, innovation)


def identity_like(matrix):
    rows = lax.broadcasted_iota(jnp.int32, matrix.shape, 0)
    cols = lax.broadcasted_iota(jnp.int32, matrix.shape, 1)
    return (rows == cols).astype(F32)


def norm_of(matrix):
    return jnp.max(jnp.sum(jnp.abs(matrix), axis=0, keepdims=True))


def scaled(error):
    square = error * error
    return 2.0 / (2.0 - square), square / (2.0 - square)


def newton_start(matrix, row, eye):
    size = matrix.shape[0]
    parts = halves(matrix)
    extended = with_row(matrix, row)
    squares = dot3(halves(extended), parts)
    square, row_moved = squares[:size], squares[size:]
    bound = jnp.sqrt(norm_of(square))
    alpha = 2.0 / (2.0 + bound)
    error0 = bound / (2.0 + bound)
    rho0, error1 = scaled(error0)
    rho1, error2 = scaled(error1)
    rest = 1.0 - alpha
    first = (rho0 * alpha) * ((2.0 - alpha) * eye - alpha * matrix)
    first_row = (rho0 * alpha) * ((2.0 - alpha) * row - alpha * row_moved)
    squared = (rest * rest) * eye - (2.0 * rest * alpha) * matrix + (alpha * alpha) * square
    residual = rho0 * squared + (1.0 - error1) * eye
    estimate = rho1 * dot3(
        halves(jnp.concatenate([first, first_row], axis=0)), halves(residual)
    )
    return estimate, error2, bound


def newton(matrices, rows, tol, eye):
    size = eye.shape[0]
    starts = [newton_start(m, r, eye) for m, r in zip(matrices, rows)]
    systems = [halves(eye + m) for m in matrices]

    def unfinished(state):
        return functools.reduce(jnp.maximum, state[1]) > tol

    def turn(state):
        new_estimates, new_errors = [], []
        for system, estimate, error in zip(systems, *state):
            parts = halves(estimate)
            residual = 2.0 * eye - dot3(system, tuple(part[:size] for part in parts))
            rho, error = scaled(error)
            new_estimates.append(rho * dot3(parts, halves(residual)))
            new_errors.append(error)
        return tuple(new_estimates), tuple(new_errors)

    state = tuple(s[0] for s in starts), tuple(s[1] for s in starts)
    estimates, unused = lax.while_loop(unfinished, turn, state)
    return estimates, functools.reduce(jnp.maximum, [s[2] for s in starts])


def invert_shifted(matrices, rows):
    eye = identity_like(matrices[0])
    size = eye.shape[0]
    estimates, bound = newton(matrices, rows, 0.03, eye)
    turns = jnp.where(bound > 300.0, 4, 1)

    def polish(index, estimates):
        result = []
        for m, estimate in zip(matrices, estimates):
            inverse = estimate[:size]
            residual = eye - inverse - dot6(m, inverse)
            rough = residual.astype(BF16)
            change = residual + dot1(rough, rough)
            result.append(estimate + dot3(halves(estimate), halves(change)))
        return tuple(result)

    estimates = lax.fori_loop(0, turns, polish, estimates)
    return [(e[:size], e[size : size + 1]) for e in estimates]


def column(row):
    size = row.shape[1]
    return jnp.broadcast_to(row, (size, size)).T


def pair_kernel(
    full, mine_ref, other_ref, transition_ref, model_error_ref,
    a_ref, j_ref, vec_ref, prefix_ref, *more,
):
    window = lax.axis_index("tm")
    lower_core = lax.rem(window, 2) == 0
    moves = jnp.where(window < 2, 0.0, 1.0)
    mine, other = mine_ref[...], other_ref[...]
    q2 = model_error_ref[...]
    size = q2.shape[1]
    root_row = jnp.sqrt(q2)
    root_col = column(root_row)
    transition = transition_ref[...]
    weighted = transition / column(q2)
    turned = halves(weighted.T)
    weighted = halves(weighted)
    mats, rows = [], []
    for packed in (jnp.where(lower_core, mine, other), jnp.where(lower_core, other, mine)):
        matrix, vector = load_packed(packed)
        mats.append(root_col * matrix * root_row)
        rows.append(root_row * vector)
    (p1, r1), (p2, r2) = invert_shifted(mats, rows)
    c1, b1 = root_col * p1 * root_row, r1 * root_row
    c2, b2 = root_col * p2 * root_row, r2 * root_row
    low = halves(with_row(c1, b1))
    a1 = moves * dot3(low, weighted)
    a2 = dot3(halves(with_row(c2, b2)), weighted)
    k1 = dot3(low, turned)
    a1, eta1 = a1[:size], a1[size : size + 1]
    a2, eta2 = a2[:size], a2[size : size + 1]
    rest2 = halves(transition - a2)
    crossed = dot3(halves(k1), rest2)
    j2 = dot3(turned, rest2)
    j1 = moves * dot3(turned, halves(transition - a1))
    outer = dot3(low, halves(a2), NT)
    spread = dot3(halves(a1.T), halves(j2))
    ((inverse, s),) = invert_shifted([crossed[:size]], [eta2 - crossed[size : size + 1]])
    both = jnp.concatenate([a1, outer[:size]], axis=1)
    middle = dot3(halves(with_row(inverse, s)), halves(both))
    right = halves(middle[:size])
    ended = dot3(halves(a2), right)
    trans, cov = ended[:, :size], ended[:, size:] + c2
    prec = dot3(halves(spread), tuple(part[:, :size] for part in right)) + j1
    info = middle[size : size + 1, :size] + eta1
    mean = outer[size : size + 1] + middle[size : size + 1, size:] + b2
    a_ref[...] = jnp.where(lower_core, a1, trans)
    j_ref[...] = jnp.where(lower_core, j1, prec)
    vec_ref[0:1] = jnp.where(lower_core, b1, mean)
    vec_ref[1:2] = jnp.where(lower_core, eta1, info)
    vec_ref[2:3] = mean
    vec_ref[3:4] = info
    vec_ref[4:SUB] = jnp.zeros((SUB - 4, size), F32)
    store_packed(prefix_ref, cov, mean)
    if full:
        for ref, value in zip(more, (trans, prec, cov)):
            ref[...] = value


def pair_up(mine, other, transition, model_error, full):
    order = transition.shape[0]
    square = jax.ShapeDtypeStruct((order, order), F32)
    shapes = [
        square,
        square,
        jax.ShapeDtypeStruct((SUB, order), F32),
        jax.ShapeDtypeStruct(mine.shape, F32),
    ] + [square] * (3 if full else 0)
    return pl.pallas_call(
        functools.partial(pair_kernel, full),
        out_shape=shapes,
        in_specs=[VMEM] * 4,
        out_specs=[VMEM] * len(shapes),
        compiler_params=params(24),
        name="pair_up",
    )(mine, other, transition, model_error)


def advance_kernel(incoming_ref, a_ref, j_ref, c_ref, vec_ref, out_ref):
    cov0, mean0 = load_packed(incoming_ref[...])
    size = mean0.shape[1]
    low = halves(with_row(cov0, mean0))
    crossed = dot3(low, halves(j_ref[...]))
    outer = dot3(low, halves(a_ref[...]), NT)
    ((inverse, s),) = invert_shifted(
        [crossed[:size]], [vec_ref[3:4] - crossed[size : size + 1]]
    )
    middle = dot3(halves(with_row(inverse, s)), halves(outer[:size]))
    mean = outer[size : size + 1] + middle[size : size + 1] + vec_ref[2:3]
    cov = dot3(halves(a_ref[...]), halves(middle[:size])) + c_ref[...]
    store_packed(out_ref, cov, mean)


def advance_prefix(incoming, a, j, c, vec):
    return pl.pallas_call(
        advance_kernel,
        out_shape=jax.ShapeDtypeStruct(incoming.shape, F32),
        in_specs=[VMEM] * 5,
        out_specs=VMEM,
        compiler_params=params(16),
        name="advance_prefix",
    )(incoming, a, j, c, vec)


def finish_kernel(rows, nx, incoming_ref, a_ref, j_ref, vec_ref, basis_ref, mean_ref, sum_ref):
    moves = jnp.where(lax.axis_index("tm") < 2, 0.0, 1.0)
    cov0, mean0 = load_packed(incoming_ref[...] * moves)
    size = mean0.shape[1]
    eye = identity_like(cov0)
    crossed = dot3(halves(with_row(cov0, mean0)), halves(j_ref[...]))
    matrix = crossed[:size]
    target = jnp.broadcast_to(vec_ref[1:2], (SUB, size)) - crossed[size:]
    (estimate,), bound = newton([matrix], [target[0:1]], 0.03, eye)
    parts = halves(matrix)
    inverse = halves(estimate[:size])

    def polish(index, s):
        miss = target - s - dot3(halves(s), parts)
        return s + dot3(halves(miss), inverse)

    s = lax.fori_loop(0, jnp.where(bound > 300.0, 8, 3), polish, estimate[size:])
    ahead = mean0 + dot3(halves(s), halves(cov0))
    mean = (dot3(halves(ahead), halves(a_ref[...]), NT) + vec_ref[0:1])[0:1]
    mean_ref[...] = mean
    pieces = jnp.concatenate(list(thirds(mean)) + [jnp.zeros((5, size), BF16)], axis=0)
    sums = dot1(pieces, basis_ref[...])
    total = sums[0:1] + (sums[1:2] + sums[2:3])
    for i in range(3 * rows):
        sum_ref[i : i + 1, :] = total[:, i * nx : (i + 1) * nx]


def finish(incoming, a, j, vec, basis, rows, nx):
    order = a.shape[0]
    return pl.pallas_call(
        functools.partial(finish_kernel, rows, nx),
        out_shape=[
            jax.ShapeDtypeStruct((1, order), F32),
            jax.ShapeDtypeStruct((3 * rows, nx), F32),
        ],
        in_specs=[VMEM] * 5,
        out_specs=[VMEM] * 2,
        compiler_params=params(16),
        name="finish",
    )(incoming, a, j, vec, basis)


def increments_kernel(rows, nx, own_ref, first_ref, second_ref, mo, mf, ms, out_ref):
    tile, tiles = lax.axis_index("tile"), lax.axis_size("tile")

    def extend(own, first, second):
        before, after = before_after(first, second)
        return jnp.concatenate([before, own, after], axis=0)

    depth = extend(mo[0:rows, :], mf[0:rows, :], ms[0:rows, :]) * B_COEF
    h, u, v = [
        extend(*(ref[f * rows : (f + 1) * rows, :] for ref in (own_ref, first_ref, second_ref)))
        for f in range(3)
    ]
    total = 3 * rows
    y_iota = lax.broadcasted_iota(jnp.int32, (total, nx), 0)
    first_row = jnp.where(tile == 0, rows, 0)
    last_row = jnp.where(tile == tiles - 1, 2 * rows, total)
    inside = ((y_iota >= first_row) & (y_iota < last_row)).astype(F32)

    def diff_cols(values):
        return pltpu.roll(values, nx - 1, 1) - pltpu.roll(values, 1, 1)

    def diff_rows(values):
        return pltpu.roll(values, total - 1, 0) - pltpu.roll(values, 1, 0)

    for step in range(STEPS):
        east = u + CORIOLIS * v - A_COEF * diff_cols(h)
        north = (v - CORIOLIS * u - A_COEF * diff_rows(h)) * inside
        h = h - depth * (diff_cols(east) + diff_rows(north))
        u, v = east, north
    for f, values in enumerate((h, u, v)):
        out_ref[f] = values[rows : 2 * rows]


def propagate_sum(own, first, second, mo, mf, ms, rows, nx):
    return pl.pallas_call(
        functools.partial(increments_kernel, rows, nx),
        out_shape=jax.ShapeDtypeStruct((3, rows, nx), F32),
        in_specs=[VMEM] * 6,
        out_specs=VMEM,
        compiler_params=params(8),
        name="propagate_sum",
    )(own, first, second, mo, mf, ms)


def info_kernel(depth_ref, cells_ref, fields_ref, out_ref):
    rows = depth_ref.shape[0]
    out_ref[0:rows, :] = depth_ref[...]
    out_ref[rows : 2 * rows, :] = jnp.zeros_like(depth_ref)
    out_ref[rows : rows + 1, :] = cells_ref[...].astype(F32)
    out_ref[rows + 1 : rows + 2, :] = fields_ref[...].astype(F32)


def gather_info(mean_depth, obs_cells, obs_fields):
    rows, nx = mean_depth.shape
    return pl.pallas_call(
        info_kernel,
        out_shape=jax.ShapeDtypeStruct((2 * rows, nx), F32),
        in_specs=[VMEM] * 3,
        out_specs=VMEM,
        compiler_params=params(4),
        name="gather_info",
    )(mean_depth, obs_cells, obs_fields)


def on_device(
    basis_fields, mean_depth, obs_cells, obs_fields, obs_weight, innovation, transition, model_error
):
    order, rows, nx = basis_fields.shape[2:]
    tiles = lax.axis_size("tile")
    windows = lax.axis_size("tm")
    near = [(i, i ^ 1) for i in range(tiles)]
    across = [i if i in (0, tiles - 1) else (i + 1 if i % 2 else i - 1) for i in range(tiles)]
    far = [
        (w * tiles + i, (w ^ 1 if across[i] == i else w) * tiles + across[i])
        for w in range(windows)
        for i in range(tiles)
    ]

    def swap_near(array):
        return lax.ppermute(array, "tile", near)

    def swap_far(array):
        return lax.ppermute(array, ("tm", "tile"), far)

    info = gather_info(mean_depth, obs_cells, obs_fields)
    info_near = swap_near(info)
    basis = basis_fields[0].transpose(1, 0, 2, 3).reshape(order, 3 * rows * nx)
    info_later, basis = lax.optimization_barrier((info, basis))
    info_far = swap_far(info_later)

    part_near = project(NEAR, info, info_near, info_near, basis, rows, nx)
    got_near = swap_near(part_near)
    part_far = project(FAR, info, info_far, info_far, basis, rows, nx)
    got_far = swap_far(part_far)
    part_own = project(OWN, info, info_near, info_far, basis, rows, nx)

    packed = gram(part_own, got_near, got_far, obs_weight, innovation)
    bit = 1
    while bit < tiles:
        packed = packed + lax.ppermute(packed, "tile", [(i, i ^ bit) for i in range(tiles)])
        bit *= 2

    other = lax.ppermute(packed, "tm", [(i, i ^ 1) for i in range(windows)])
    pairs = windows // 2
    a, j, vec, prefix, *more = pair_up(
        packed, other, transition, model_error[None, :], pairs > 2
    )
    incoming = jnp.zeros_like(prefix)
    pair = lax.axis_index("tm") // 2
    for turn in range(pairs - 1):
        if pairs == 2:
            hop = [(i, i ^ 2) for i in range(windows)]
        else:
            hop = [(i, i + 2) for i in range(windows - 2)]
        incoming = lax.ppermute(prefix, "tm", hop)
        if turn < pairs - 2:
            longer = advance_prefix(incoming, *more, vec)
            prefix = jnp.where(pair == turn + 1, longer, prefix)
    mean, sums = finish(incoming, a, j, vec, basis, rows, nx)
    result = propagate_sum(
        sums, swap_near(sums), swap_far(sums), info, info_near, info_far, rows, nx
    )
    return mean, result[None]


def solution(mesh):
    return jax.shard_map(
        on_device,
        mesh=mesh,
        in_specs=(
            P("tm", None, None, "tile", None),
            P("tile", None),
            P("tm", "tile"),
            P("tm", "tile"),
            P("tm", "tile"),
            P("tm", "tile"),
            P(),
            P(),
        ),
        out_specs=(P("tm", None), P("tm", None, "tile", None)),
        check_vma=False,
    )
```

```python
import functools

import jax
import jax.numpy as jnp
from jax import lax
from jax.experimental import pallas as pl
from jax.experimental.pallas import tpu as pltpu
from jax.sharding import PartitionSpec as P


STEPS = 4
A_COEF = 0.5
B_COEF = 0.5
CORIOLIS = 0.3

F32 = jnp.float32
BF16 = jnp.bfloat16
LANES = 128
SUB = 8
REACH = 2 * STEPS
PADX = REACH + 1
NEAR, FAR, OWN = "project_near", "project_far", "project_own"
FINE = 16
NARROW = 16.0
HIGH = lax.Precision.HIGHEST
NT = (((1,), (1,)), ((), ()))
NN = (((1,), (0,)), ((), ()))
VMEM = pl.BlockSpec(memory_space=pltpu.VMEM)


def params(mib):
    return pltpu.CompilerParams(vmem_limit_bytes=mib << 20)


def dot6(left, right, dims=NN):
    return lax.dot_general(left, right, dims, precision=HIGH, preferred_element_type=F32)


def dot1(left, right, dims=NN):
    return lax.dot_general(left, right, dims, preferred_element_type=F32)


def halves(values):
    high = values.astype(BF16)
    return high, (values - high.astype(F32)).astype(BF16)


def thirds(values):
    high = values.astype(BF16)
    rest = values - high.astype(F32)
    mid = rest.astype(BF16)
    return high, mid, (rest - mid.astype(F32)).astype(BF16)


def dot3(left, right, dims=NN):
    (lh, ll), (rh, rl) = left, right
    return dot1(lh, rh, dims) + (dot1(lh, rl, dims) + dot1(ll, rh, dims))


def before_after(first, second):
    tile, tiles = lax.axis_index("tile"), lax.axis_size("tile")
    even = lax.rem(tile, 2) == 0
    before = jnp.where(even, jnp.where(tile == 0, 0.0, second), first)
    after = jnp.where(even, first, jnp.where(tile == tiles - 1, 0.0, second))
    return before, after


def window_rows(slot, rows, even, own_ref, first_ref, second_ref):
    own = own_ref[0:rows, :] * B_COEF
    first = first_ref[0:rows, :] * B_COEF
    if slot == OWN:
        second = second_ref[0:rows, :] * B_COEF
        above, below = before_after(first, second)
        domain = jnp.concatenate([above[rows // 2 :], own, below[: rows // 2]], axis=0)
        base = rows // 2
    else:
        domain = jnp.concatenate(
            [jnp.where(even, own, first), jnp.where(even, first, own)], axis=0
        )
        base = jnp.where(even, rows, 0)
    return domain, base


def project_kernel(
    slot, rows, nx, own_ref, first_ref, second_ref, basis_ref, out_ref,
    bmw, p, g, qp, sp, w, sh, sl,
):
    own_slot = slot == OWN
    obs_ref = own_ref if own_slot else first_ref
    tile, tiles = lax.axis_index("tile"), lax.axis_size("tile")
    even = lax.rem(tile, 2) == (1 if slot == FAR else 0)
    domain, base = window_rows(slot, rows, even, own_ref, first_ref, second_ref)
    depth = 2 * rows
    nob = obs_ref.shape[1] // LANES
    inner = REACH - 2
    rolled = [
        pltpu.roll(domain, (-dx) % nx, 1) if dx else domain for dx in range(-inner, inner + 1)
    ]
    stacked = jnp.concatenate(rolled, axis=0)
    pieces = thirds(stacked)
    cells = obs_ref[rows : rows + 1, :]
    fields = obs_ref[rows + 1 : rows + 2, :]
    row_all = jnp.floor(cells * (1.0 / nx))
    col = (cells - row_all * nx).astype(jnp.int32)
    row = (row_all - rows * jnp.floor(row_all * (1.0 / rows))).astype(jnp.int32) + base
    field = fields.astype(jnp.int32)
    y_iota = lax.broadcasted_iota(jnp.int32, (depth, LANES), 0)
    x_iota = lax.broadcasted_iota(jnp.int32, (nx, LANES), 0)
    if own_slot:
        first_row = jnp.where(tile == 0, rows // 2, 0)
        last_row = jnp.where(tile == tiles - 1, rows // 2 + rows, depth)
        inside = ((y_iota >= first_row) & (y_iota < last_row)).astype(F32)
    lo, hi = SUB, SUB + depth
    zero_rows = jnp.zeros((SUB, LANES), F32)
    for ob in range(nob):
        lane = slice(ob * LANES, (ob + 1) * LANES)
        onehot = (x_iota == col[:, lane]).astype(F32).astype(BF16)
        depths = dot1(pieces[0], onehot) + (dot1(pieces[1], onehot) + dot1(pieces[2], onehot))
        for i in range(2 * inner + 1):
            bmw[ob, i] = depths[i * depth : (i + 1) * depth]
        for i in range(2 * PADX + 1):
            g[ob, i, 0:lo] = zero_rows
            g[ob, i, hi : hi + SUB] = zero_rows
            sp[ob, i, 0:lo] = zero_rows
            sp[ob, i, hi : hi + SUB] = zero_rows
        at_row = y_iota == row[:, lane]
        start = [(at_row & (field[:, lane] == f)).astype(F32) for f in range(3)]

        def at(ref, dx):
            return ref[ob, dx + PADX, lo:hi]

        def slope(ref, dx):
            return ref[ob, dx + PADX, lo + 1 : hi + 1] - ref[ob, dx + PADX, lo - 1 : hi - 1]

        p[ob, PADX, lo:hi] = start[0]
        for step in range(STEPS):
            reach = 2 * step
            for dx in range(-reach, reach + 1):
                g[ob, dx + PADX, lo:hi] = bmw[ob, dx + inner] * at(p, dx)
            for dx in range(-reach - 1, reach + 2):
                if step == 0:
                    east, north = (start[1], start[2]) if dx == 0 else (None, None)
                elif abs(dx) <= reach - 2:
                    qv, sv = at(qp, dx), at(sp, dx)
                    east, north = qv - CORIOLIS * sv, sv + CORIOLIS * qv
                elif abs(dx) == reach - 1:
                    east = at(qp, dx)
                    north = CORIOLIS * east
                else:
                    east, north = None, None
                if abs(dx + 1) <= reach:
                    east = at(g, dx + 1) if east is None else east + at(g, dx + 1)
                if abs(dx - 1) <= reach:
                    east = -at(g, dx - 1) if east is None else east - at(g, dx - 1)
                qp[ob, dx + PADX, lo:hi] = east
                if abs(dx) <= reach:
                    rise = slope(g, dx)
                    north = rise if north is None else north + rise
                    if own_slot:
                        north = north * inside
                    sp[ob, dx + PADX, lo:hi] = north
            for dx in range(-reach - 2, reach + 3):
                change = None
                if abs(dx + 1) <= reach + 1:
                    change = at(qp, dx + 1)
                if abs(dx - 1) <= reach + 1:
                    change = -at(qp, dx - 1) if change is None else change - at(qp, dx - 1)
                if abs(dx) <= reach:
                    change = change + slope(sp, dx)
                change = A_COEF * change
                if abs(dx) <= reach:
                    change = change + at(p, dx)
                p[ob, dx + PADX, lo:hi] = change

    if own_slot:
        picked = slice(lo + rows // 2, lo + rows // 2 + rows)
    else:
        picked = pl.ds(pl.multiple_of(jnp.where(even, lo, lo + rows), SUB), rows)
    zero = jnp.zeros((rows, LANES), F32)
    blocks = nx // FINE
    shift = lax.rem(col + (nx - REACH), nx)
    depth_f = rows * nx
    total = None
    for f in range(3):
        for ob in range(nob):
            lane = slice(ob * LANES, (ob + 1) * LANES)
            fine = jnp.broadcast_to(lax.rem(shift[:, lane], FINE), (rows, LANES))
            bits = [(fine & (1 << i)) != 0 for i in range(4)]
            coarse = jnp.broadcast_to(shift[:, lane] // FINE, (FINE, LANES))
            marks = [(coarse == block).astype(F32).astype(BF16) for block in range(blocks)]
            values = [None] * (2 * FINE)
            for dx in range(-REACH, REACH + 1):
                if f == 0:
                    value = p[ob, dx + PADX, picked]
                elif abs(dx) <= REACH - 2:
                    qv, sv = qp[ob, dx + PADX, picked], sp[ob, dx + PADX, picked]
                    value = qv - CORIOLIS * sv if f == 1 else sv + CORIOLIS * qv
                elif abs(dx) == REACH - 1:
                    qv = qp[ob, dx + PADX, picked]
                    value = qv if f == 1 else CORIOLIS * qv
                else:
                    value = None
                values[dx + REACH] = value
            for i in range(4):
                moved = []
                for e in range(2 * FINE):
                    here = values[e]
                    there = values[e - (1 << i)] if e >= (1 << i) else None
                    if here is None and there is None:
                        moved.append(None)
                    else:
                        moved.append(
                            jnp.where(
                                bits[i],
                                zero if there is None else there,
                                zero if here is None else here,
                            )
                        )
                values = moved
            for e in range(2 * FINE):
                w[f, ob, e * rows : (e + 1) * rows, :] = zero if values[e] is None else values[e]
            for y in range(rows):
                both = halves(w[f, ob, pl.ds(y, 2 * FINE, stride=rows), :])
                for part, ref in zip(both, (sh, sl)):
                    near, far = part[:FINE], part[FINE:]
                    for block in range(blocks):
                        start_row = (f * rows + y) * nx + block * FINE
                        ref[start_row : start_row + FINE, lane] = (
                            near * marks[block] + far * marks[block - 1]
                        )
        span = slice(f * depth_f, (f + 1) * depth_f)
        basis = basis_ref[:, span]
        part = dot1(basis, sh[span, :]) + dot1(basis, sl[span, :])
        total = part if total is None else total + part
    out_ref[...] = total


def project(slot, own, first, second, basis, rows, nx):
    order, depth_all = basis.shape
    nobs = own.shape[1]
    nob = nobs // LANES
    wide = (nob, 2 * PADX + 1, 2 * rows + 2 * SUB, LANES)
    return pl.pallas_call(
        functools.partial(project_kernel, slot, rows, nx),
        out_shape=jax.ShapeDtypeStruct((order, nobs), F32),
        in_specs=[VMEM] * 4,
        out_specs=VMEM,
        scratch_shapes=[
            pltpu.VMEM((nob, 2 * REACH - 3, 2 * rows, LANES), F32),
            pltpu.VMEM(wide, F32),
            pltpu.VMEM(wide, F32),
            pltpu.VMEM(wide, F32),
            pltpu.VMEM(wide, F32),
            pltpu.VMEM((3, nob, 2 * FINE * rows, LANES), F32),
            pltpu.VMEM((depth_all, nobs), BF16),
            pltpu.VMEM((depth_all, nobs), BF16),
        ],
        compiler_params=params(48),
        cost_estimate=pl.CostEstimate(
            flops=4 * order * depth_all * nobs,
            bytes_accessed=2 * order * depth_all,
            transcendentals=0,
        ),
    )(own, first, second, basis)


def triangle_masks(half):
    rows = lax.broadcasted_iota(jnp.int32, (half, half), 0)
    cols = lax.broadcasted_iota(jnp.int32, (half, half), 1)
    return rows, cols


def store_packed(out_ref, matrix, vector):
    half = matrix.shape[0] // 2
    rows, cols = triangle_masks(half)
    corner = matrix[half:, half:]
    out_ref[0:half] = jnp.where(rows >= cols, matrix[:half, :half], corner)
    out_ref[half : 2 * half] = matrix[half:, :half]
    diagonal = jnp.sum(jnp.where(rows == cols, corner, 0.0), axis=0, keepdims=True)
    tail = jnp.concatenate(
        [vector[:, :half], vector[:, half:], diagonal, jnp.zeros((SUB - 3, half), F32)], axis=0
    )
    out_ref[2 * half : 2 * half + SUB] = tail


def load_packed(values):
    half = values.shape[1]
    rows, cols = triangle_masks(half)
    mixed = values[0:half]
    cross = values[half : 2 * half]
    vector = jnp.concatenate(
        [values[2 * half : 2 * half + 1], values[2 * half + 1 : 2 * half + 2]], axis=1
    )
    diagonal = values[2 * half + 2 : 2 * half + 3]
    turned = mixed.T
    first = jnp.where(rows >= cols, mixed, turned)
    last = jnp.where(rows == cols, diagonal, jnp.where(rows < cols, mixed, turned))
    top = jnp.concatenate([first, cross.T], axis=1)
    bottom = jnp.concatenate([cross, last], axis=1)
    return jnp.concatenate([top, bottom], axis=0), vector


def with_row(matrix, row):
    return jnp.concatenate([matrix, jnp.broadcast_to(row, (SUB, row.shape[1]))], axis=0)


def gram_kernel(own_ref, first_ref, second_ref, weight_ref, innovation_ref, out_ref):
    tile, tiles = lax.axis_index("tile"), lax.axis_size("tile")
    inner = (tile != 0) & (tile != tiles - 1)
    projected = own_ref[...] + first_ref[...] + jnp.where(inner, second_ref[...], 0.0)
    weight = weight_ref[...]
    left = with_row(projected * weight, weight * innovation_ref[...])
    result = dot3(halves(left), halves(projected), NT)
    size = projected.shape[0]
    store_packed(out_ref, result[:size], result[size : size + 1])


def gram(own, first, second, weight, innovation):
    order = own.shape[0]
    return pl.pallas_call(
        gram_kernel,
        out_shape=jax.ShapeDtypeStruct((order + SUB, order // 2), F32),
        in_specs=[VMEM] * 5,
        out_specs=VMEM,
        compiler_params=params(8),
        name="gram",
    )(own, first, second, weight, innovation)


def identity_like(matrix):
    rows = lax.broadcasted_iota(jnp.int32, matrix.shape, 0)
    cols = lax.broadcasted_iota(jnp.int32, matrix.shape, 1)
    return (rows == cols).astype(F32)


def norm_of(matrix):
    sums = jnp.sum(jnp.abs(matrix), axis=0, keepdims=True)
    return jnp.broadcast_to(jnp.max(sums, axis=1, keepdims=True), sums.shape)


def scaled(error):
    square = error * error
    rho = 2.0 / (2.0 - square)
    return rho, 0.5 * square * rho


def chebyshev_start(matrix, square, eye):
    bound = jnp.sqrt(norm_of(square))
    alpha = 2.0 / (2.0 + bound)
    error0 = 0.5 * bound * alpha
    rho, error = scaled(error0)
    rest = 1.0 - alpha
    factor = rho * alpha
    residual = rho * (
        (rest * rest) * eye - (2.0 * rest * alpha) * matrix + (alpha * alpha) * square
    ) - error * eye
    return factor * (2.0 - alpha), factor * alpha, residual, error, bound


def rough_turns(state, eye):
    size = eye.shape[0]
    new = []
    for estimate, residual, error in state:
        rho, error = scaled(error)
        part = residual.astype(BF16)
        moved = dot1(jnp.concatenate([estimate.astype(BF16), part], axis=0), part)
        new.append((rho * (estimate + moved[:size]), rho * moved[size:] - error * eye, error))
    return new


def polish(matrix, part, estimate, eye, exact):
    pieces = halves(estimate)
    moved = dot6(matrix, estimate) if exact else dot3(part, pieces)
    residual = eye - estimate - moved
    rough = residual.astype(BF16)
    change = residual + dot1(rough, rough)
    return estimate + dot3(pieces, halves(change))


def invert_any(matrix, part, c0, c1, error, eye):
    def unsure(state):
        return jnp.max(state[1]) > 0.03

    def turn(state):
        estimate, error = state
        pieces = halves(estimate)
        residual = 2.0 * eye - estimate - dot3(part, pieces)
        rho, error = scaled(error)
        return rho * dot3(pieces, halves(residual)), error

    estimate, error = lax.while_loop(unsure, turn, (c0 * eye - c1 * matrix, error))
    return lax.fori_loop(
        0, 4, lambda index, value: polish(matrix, part, value, eye, True), estimate
    )


def invert_shifted(matrices, parts, turns):
    eye = identity_like(matrices[0])
    state, starts, bounds = [], [], []
    for matrix, part in zip(matrices, parts):
        square = dot1(part[0], part[0])
        c0, c1, residual, error, bound = chebyshev_start(matrix, square, eye)
        state.append((c0 * eye - c1 * matrix, residual, error))
        starts.append((c0, c1, error))
        bounds.append(bound)
    narrow = jnp.max(functools.reduce(jnp.maximum, bounds)) < NARROW
    for _ in range(turns):
        state = rough_turns(state, eye)
    last = functools.reduce(jnp.maximum, [one[2] for one in state])
    enough = narrow & (jnp.max(last) < 0.04)
    quick = tuple(
        polish(m, part, one[0], eye, False) for m, part, one in zip(matrices, parts, state)
    )

    def careful():
        return tuple(
            invert_any(m, part, *start, eye) for m, part, start in zip(matrices, parts, starts)
        )

    return lax.cond(enough, lambda: quick, careful)


def solve_shifted(matrix, parts, row):
    eye = identity_like(matrix)
    row_parts = halves(row)
    extended = tuple(jnp.concatenate(two, axis=0) for two in zip(row_parts, parts))
    squares = dot3(extended, parts)
    moved, square = squares[:SUB], squares[SUB:]
    c0, c1, residual, error, _ = chebyshev_start(matrix, square, eye)
    rho, last = scaled(error)
    part = halves(residual)
    start = c0 * row - c1 * moved
    both = tuple(jnp.concatenate(two, axis=0) for two in zip(halves(start), part))
    moved = dot3(both, part)
    current = rho * (start + moved[:SUB])
    part = halves(rho * moved[SUB:] - last * eye)
    once = dot3(halves(current), part)
    quick = current + once + dot3(halves(once), part)

    def careful():
        inverse = invert_any(matrix, parts, c0, c1, error, eye)
        pieces = halves(inverse)

        def correct(index, value):
            miss = row - value - dot6(value, matrix)
            return value + dot3(halves(miss), pieces)

        return lax.fori_loop(0, 3, correct, dot3(row_parts, pieces))

    return lax.cond(jnp.max(last) < 0.03, lambda: quick, careful)


def column(row):
    size = row.shape[1]
    return jnp.broadcast_to(row, (size, size)).T


def row_dot(row, parts, dims=NN):
    return dot3(halves(jnp.broadcast_to(row, (SUB, row.shape[1]))), parts, dims)[0:1]


def pair_kernel(
    full, mine_ref, other_ref, transition_ref, model_error_ref,
    a_ref, j_ref, vec_ref, prefix_ref, *more,
):
    window = lax.axis_index("tm")
    lower_core = lax.rem(window, 2) == 0
    moves = jnp.where(window < 2, 0.0, 1.0)
    mine, other = mine_ref[...], other_ref[...]
    q2 = model_error_ref[...]
    size = q2.shape[1]
    root_row = jnp.sqrt(q2)
    root_col = column(root_row)
    transition = transition_ref[...]
    weighted = transition / column(q2)
    turned = halves(weighted.T)
    weighted = halves(weighted)
    mats, rows = [], []
    for packed in (jnp.where(lower_core, mine, other), jnp.where(lower_core, other, mine)):
        matrix, vector = load_packed(packed)
        mats.append(root_col * matrix * root_row)
        rows.append(root_row * vector)
    p1, p2 = invert_shifted(mats, [halves(m) for m in mats], 2)
    c1, c2 = root_col * p1 * root_row, root_col * p2 * root_row
    low = halves(c1)
    a2 = dot3(halves(c2), weighted)
    k1 = dot3(low, turned)
    rest2 = halves(transition - a2)
    crossed = dot3(halves(k1), rest2)
    a1 = moves * dot3(low, weighted)
    b1 = row_dot(rows[0], halves(p1)) * root_row
    b2 = row_dot(rows[1], halves(p2)) * root_row
    eta1 = moves * row_dot(b1, weighted)
    eta2 = row_dot(b2, weighted)
    j2 = dot3(turned, rest2)
    j1 = moves * dot3(turned, halves(transition - a1))
    a2_parts = halves(a2)
    a1_parts = halves(a1)
    j2_parts = halves(j2)
    outer = dot3(low, a2_parts, NT)
    ahead = row_dot(b1, a2_parts, NT) + b2
    behind = eta2 - row_dot(b1, j2_parts)
    spread = dot3(halves(a1.T), j2_parts)
    (inverse,) = invert_shifted([crossed], [halves(crossed)], 1)
    inverse = halves(inverse)
    both = tuple(
        jnp.concatenate(two, axis=1) for two in zip(a1_parts, halves(outer))
    )
    right = halves(dot3(inverse, both))
    s = row_dot(behind, inverse)
    ended = dot3(a2_parts, right)
    ended_rows = row_dot(s, both)
    trans, cov = ended[:, :size], ended[:, size:] + c2
    prec = dot3(halves(spread), tuple(part[:, :size] for part in right)) + j1
    info = ended_rows[:, :size] + eta1
    mean = ended_rows[:, size:] + ahead
    a_ref[...] = jnp.where(lower_core, a1, trans)
    j_ref[...] = jnp.where(lower_core, j1, prec)
    vec_ref[0:1] = jnp.where(lower_core, b1, mean)
    vec_ref[1:2] = jnp.where(lower_core, eta1, info)
    vec_ref[2:3] = mean
    vec_ref[3:4] = info
    vec_ref[4:SUB] = jnp.zeros((SUB - 4, size), F32)
    store_packed(prefix_ref, cov, mean)
    if full:
        for ref, value in zip(more, (trans, prec, cov)):
            ref[...] = value


def pair_up(mine, other, transition, model_error, full):
    order = transition.shape[0]
    square = jax.ShapeDtypeStruct((order, order), F32)
    shapes = [
        square,
        square,
        jax.ShapeDtypeStruct((SUB, order), F32),
        jax.ShapeDtypeStruct(mine.shape, F32),
    ] + [square] * (3 if full else 0)
    return pl.pallas_call(
        functools.partial(pair_kernel, full),
        out_shape=shapes,
        in_specs=[VMEM] * 4,
        out_specs=[VMEM] * len(shapes),
        compiler_params=params(24),
        name="pair_up",
    )(mine, other, transition, model_error)


def advance_kernel(incoming_ref, a_ref, j_ref, c_ref, vec_ref, out_ref):
    cov0, mean0 = load_packed(incoming_ref[...])
    low = halves(cov0)
    forward = halves(a_ref[...])
    back = halves(j_ref[...])
    crossed = dot3(low, back)
    outer = halves(dot3(low, forward, NT))
    behind = vec_ref[3:4] - row_dot(mean0, back)
    (inverse,) = invert_shifted([crossed], [halves(crossed)], 1)
    inverse = halves(inverse)
    s = row_dot(behind, inverse)
    mean = row_dot(mean0, forward, NT) + row_dot(s, outer) + vec_ref[2:3]
    cov = dot3(forward, halves(dot3(inverse, outer))) + c_ref[...]
    store_packed(out_ref, cov, mean)


def advance_prefix(incoming, a, j, c, vec):
    return pl.pallas_call(
        advance_kernel,
        out_shape=jax.ShapeDtypeStruct(incoming.shape, F32),
        in_specs=[VMEM] * 5,
        out_specs=VMEM,
        compiler_params=params(16),
        name="advance_prefix",
    )(incoming, a, j, c, vec)


def finish_kernel(rows, nx, incoming_ref, a_ref, j_ref, vec_ref, basis_ref, mean_ref, sum_ref):
    moves = jnp.where(lax.axis_index("tm") < 2, 0.0, 1.0)
    cov0, mean0 = load_packed(incoming_ref[...] * moves)
    size = mean0.shape[1]
    low = halves(with_row(cov0, mean0))
    crossed = dot3(low, halves(j_ref[...]))
    outer = dot3(low, halves(a_ref[...]), NT)
    matrix = crossed[:size]
    target = jnp.broadcast_to(vec_ref[1:2], (SUB, size)) - crossed[size:]
    s = solve_shifted(matrix, halves(matrix), target)
    mean = (dot3(halves(s), halves(outer[:size])) + outer[size:] + vec_ref[0:1])[0:1]
    mean_ref[...] = mean
    pieces = jnp.concatenate(list(thirds(mean)) + [jnp.zeros((5, size), BF16)], axis=0)
    for f in range(3):
        sums = dot1(pieces, basis_ref[:, f * rows * nx : (f + 1) * rows * nx])
        total = sums[0:1] + (sums[1:2] + sums[2:3])
        for y in range(rows):
            i = f * rows + y
            sum_ref[i : i + 1, :] = total[:, y * nx : (y + 1) * nx]


def finish(incoming, a, j, vec, basis, rows, nx):
    order = a.shape[0]
    return pl.pallas_call(
        functools.partial(finish_kernel, rows, nx),
        out_shape=[
            jax.ShapeDtypeStruct((1, order), F32),
            jax.ShapeDtypeStruct((3 * rows, nx), F32),
        ],
        in_specs=[VMEM] * 5,
        out_specs=[VMEM] * 2,
        compiler_params=params(16),
        name="finish",
    )(incoming, a, j, vec, basis)


def increments_kernel(rows, nx, own_ref, first_ref, second_ref, mo, mf, ms, out_ref):
    tile, tiles = lax.axis_index("tile"), lax.axis_size("tile")

    def extend(own, first, second):
        before, after = before_after(first, second)
        return jnp.concatenate([before, own, after], axis=0)

    depth = extend(mo[0:rows, :], mf[0:rows, :], ms[0:rows, :]) * B_COEF
    h, u, v = [
        extend(*(ref[f * rows : (f + 1) * rows, :] for ref in (own_ref, first_ref, second_ref)))
        for f in range(3)
    ]
    total = 3 * rows
    y_iota = lax.broadcasted_iota(jnp.int32, (total, nx), 0)
    first_row = jnp.where(tile == 0, rows, 0)
    last_row = jnp.where(tile == tiles - 1, 2 * rows, total)
    inside = ((y_iota >= first_row) & (y_iota < last_row)).astype(F32)

    def diff_cols(values):
        return pltpu.roll(values, nx - 1, 1) - pltpu.roll(values, 1, 1)

    def diff_rows(values):
        return pltpu.roll(values, total - 1, 0) - pltpu.roll(values, 1, 0)

    for _ in range(STEPS):
        east = u + CORIOLIS * v - A_COEF * diff_cols(h)
        north = (v - CORIOLIS * u - A_COEF * diff_rows(h)) * inside
        h = h - depth * (diff_cols(east) + diff_rows(north))
        u, v = east, north
    for f, values in enumerate((h, u, v)):
        out_ref[f] = values[rows : 2 * rows]


def propagate_sum(own, first, second, mo, mf, ms, rows, nx):
    return pl.pallas_call(
        functools.partial(increments_kernel, rows, nx),
        out_shape=jax.ShapeDtypeStruct((3, rows, nx), F32),
        in_specs=[VMEM] * 6,
        out_specs=VMEM,
        compiler_params=params(8),
        name="propagate_sum",
    )(own, first, second, mo, mf, ms)


def info_kernel(depth_ref, cells_ref, fields_ref, out_ref, cells, fields, sems):
    rows = depth_ref.shape[0]
    copies = [
        pltpu.make_async_copy(source, target, sems.at[i])
        for i, (source, target) in enumerate((
            (depth_ref, out_ref.at[0:rows]), (cells_ref, cells), (fields_ref, fields),
        ))
    ]
    for copy in copies:
        copy.start()
    out_ref[rows : 2 * rows, :] = jnp.zeros(depth_ref.shape, F32)
    for copy in copies:
        copy.wait()
    out_ref[rows : rows + 1, :] = cells[...].astype(F32)
    out_ref[rows + 1 : rows + 2, :] = fields[...].astype(F32)


def gather_info(mean_depth, obs_cells, obs_fields):
    rows, nx = mean_depth.shape
    return pl.pallas_call(
        info_kernel,
        out_shape=jax.ShapeDtypeStruct((2 * rows, nx), F32),
        in_specs=[pl.BlockSpec(memory_space=pl.ANY)] * 3,
        out_specs=VMEM,
        scratch_shapes=[
            pltpu.VMEM(obs_cells.shape, jnp.int32),
            pltpu.VMEM(obs_fields.shape, jnp.int32),
            pltpu.SemaphoreType.DMA((3,)),
        ],
        compiler_params=params(60),
        name="gather_info",
    )(mean_depth, obs_cells, obs_fields)


def on_device(
    basis_fields, mean_depth, obs_cells, obs_fields, obs_weight, innovation, transition, model_error
):
    order, rows, nx = basis_fields.shape[2:]
    tiles = lax.axis_size("tile")
    windows = lax.axis_size("tm")
    near = [(i, i ^ 1) for i in range(tiles)]
    across = [i if i in (0, tiles - 1) else (i + 1 if i % 2 else i - 1) for i in range(tiles)]
    far = [
        (w * tiles + i, (w ^ 1 if across[i] == i else w) * tiles + across[i])
        for w in range(windows)
        for i in range(tiles)
    ]

    def swap_near(array):
        return lax.ppermute(array, "tile", near)

    def swap_far(array):
        return lax.ppermute(array, ("tm", "tile"), far)

    info = gather_info(mean_depth, obs_cells, obs_fields)
    info_near = swap_near(info)
    info_far = swap_far(info)
    basis = basis_fields[0].transpose(1, 0, 2, 3).reshape(order, 3 * rows * nx)

    part_near = project(NEAR, info, info_near, info_near, basis, rows, nx)
    got_near = swap_near(part_near)
    info_far, unused = lax.optimization_barrier((info_far, part_near))
    part_far = project(FAR, info, info_far, info_far, basis, rows, nx)
    got_far = swap_far(part_far)
    info_own, unused = lax.optimization_barrier((info, part_far))
    part_own = project(OWN, info_own, info_near, info_far, basis, rows, nx)

    packed = gram(part_own, got_near, got_far, obs_weight, innovation)
    bit = 1
    while bit < tiles:
        packed = packed + lax.ppermute(packed, "tile", [(i, i ^ bit) for i in range(tiles)])
        bit *= 2

    other = lax.ppermute(packed, "tm", [(i, i ^ 1) for i in range(windows)])
    pairs = windows // 2
    a, j, vec, prefix, *more = pair_up(
        packed, other, transition, model_error[None, :], pairs > 2
    )
    incoming = jnp.zeros_like(prefix)
    pair = lax.axis_index("tm") // 2
    for turn in range(pairs - 1):
        if pairs == 2:
            hop = [(i, i ^ 2) for i in range(windows)]
        else:
            hop = [(i, i + 2) for i in range(windows - 2)]
        incoming = lax.ppermute(prefix, "tm", hop)
        if turn < pairs - 2:
            longer = advance_prefix(incoming, *more, vec)
            prefix = jnp.where(pair == turn + 1, longer, prefix)
    mean, sums = finish(incoming, a, j, vec, basis, rows, nx)
    sums_near = swap_near(sums)
    sums_far = swap_far(sums)
    result = propagate_sum(sums, sums_near, sums_far, info, info_near, info_far, rows, nx)
    return mean, result[None]


def solution(mesh):
    return jax.shard_map(
        on_device,
        mesh=mesh,
        in_specs=(
            P("tm", None, None, "tile", None),
            P("tile", None),
            P("tm", "tile"),
            P("tm", "tile"),
            P("tm", "tile"),
            P("tm", "tile"),
            P(),
            P(),
        ),
        out_specs=(P("tm", None), P("tm", None, "tile", None)),
        check_vma=False,
    )
```

```python
import functools

import jax
import jax.numpy as jnp
from jax import lax
from jax.experimental import pallas as pl
from jax.experimental.pallas import tpu as pltpu
from jax.sharding import PartitionSpec as P


STEPS = 4
A_COEF = 0.5
B_COEF = 0.5
CORIOLIS = 0.3

F32 = jnp.float32
BF16 = jnp.bfloat16
LANES = 128
SUB = 8
REACH = 2 * STEPS
PADX = REACH + 1
NEAR, FAR, OWN = "project_near", "project_far", "project_own"
FINE = 16
NARROW = 16.0
HIGH = lax.Precision.HIGHEST
NT = (((1,), (1,)), ((), ()))
NN = (((1,), (0,)), ((), ()))
VMEM = pl.BlockSpec(memory_space=pltpu.VMEM)


def params(mib):
    return pltpu.CompilerParams(vmem_limit_bytes=mib << 20)


def dot6(left, right, dims=NN):
    return lax.dot_general(left, right, dims, precision=HIGH, preferred_element_type=F32)


def dot1(left, right, dims=NN):
    return lax.dot_general(left, right, dims, preferred_element_type=F32)


def halves(values):
    high = values.astype(BF16)
    return high, (values - high.astype(F32)).astype(BF16)


def thirds(values):
    high = values.astype(BF16)
    rest = values - high.astype(F32)
    mid = rest.astype(BF16)
    return high, mid, (rest - mid.astype(F32)).astype(BF16)


def dot3(left, right, dims=NN):
    (lh, ll), (rh, rl) = left, right
    return dot1(lh, rh, dims) + (dot1(lh, rl, dims) + dot1(ll, rh, dims))


def before_after(first, second):
    tile, tiles = lax.axis_index("tile"), lax.axis_size("tile")
    even = lax.rem(tile, 2) == 0
    before = jnp.where(even, jnp.where(tile == 0, 0.0, second), first)
    after = jnp.where(even, first, jnp.where(tile == tiles - 1, 0.0, second))
    return before, after


def window_rows(slot, rows, even, own_ref, first_ref, second_ref):
    own = own_ref[0:rows, :] * B_COEF
    first = first_ref[0:rows, :] * B_COEF
    if slot == OWN:
        second = second_ref[0:rows, :] * B_COEF
        above, below = before_after(first, second)
        domain = jnp.concatenate([above[rows // 2 :], own, below[: rows // 2]], axis=0)
        base = rows // 2
    else:
        domain = jnp.concatenate(
            [jnp.where(even, own, first), jnp.where(even, first, own)], axis=0
        )
        base = jnp.where(even, rows, 0)
    return domain, base


def project_kernel(
    slot, rows, nx, own_ref, first_ref, second_ref, basis_ref, out_ref,
    bmw, p, g, qp, sp, w, sh, sl,
):
    own_slot = slot == OWN
    obs_ref = own_ref if own_slot else first_ref
    tile, tiles = lax.axis_index("tile"), lax.axis_size("tile")
    even = lax.rem(tile, 2) == (1 if slot == FAR else 0)
    domain, base = window_rows(slot, rows, even, own_ref, first_ref, second_ref)
    depth = 2 * rows
    nob = obs_ref.shape[1] // LANES
    inner = REACH - 2
    rolled = [
        pltpu.roll(domain, (-dx) % nx, 1) if dx else domain for dx in range(-inner, inner + 1)
    ]
    stacked = jnp.concatenate(rolled, axis=0)
    pieces = thirds(stacked)
    cells = obs_ref[rows : rows + 1, :]
    fields = obs_ref[rows + 1 : rows + 2, :]
    row_all = jnp.floor(cells * (1.0 / nx))
    col = (cells - row_all * nx).astype(jnp.int32)
    row = (row_all - rows * jnp.floor(row_all * (1.0 / rows))).astype(jnp.int32) + base
    field = fields.astype(jnp.int32)
    y_iota = lax.broadcasted_iota(jnp.int32, (depth, LANES), 0)
    x_iota = lax.broadcasted_iota(jnp.int32, (nx, LANES), 0)
    if own_slot:
        first_row = jnp.where(tile == 0, rows // 2, 0)
        last_row = jnp.where(tile == tiles - 1, rows // 2 + rows, depth)
        inside = ((y_iota >= first_row) & (y_iota < last_row)).astype(F32)
    lo, hi = SUB, SUB + depth
    zero_rows = jnp.zeros((SUB, LANES), F32)
    for ob in range(nob):
        lane = slice(ob * LANES, (ob + 1) * LANES)
        onehot = (x_iota == col[:, lane]).astype(F32).astype(BF16)
        depths = dot1(pieces[0], onehot) + (dot1(pieces[1], onehot) + dot1(pieces[2], onehot))
        for i in range(2 * inner + 1):
            bmw[ob, i] = depths[i * depth : (i + 1) * depth]
        for i in range(2 * PADX + 1):
            g[ob, i, 0:lo] = zero_rows
            g[ob, i, hi : hi + SUB] = zero_rows
            sp[ob, i, 0:lo] = zero_rows
            sp[ob, i, hi : hi + SUB] = zero_rows
        at_row = y_iota == row[:, lane]
        start = [(at_row & (field[:, lane] == f)).astype(F32) for f in range(3)]

        def at(ref, dx):
            return ref[ob, dx + PADX, lo:hi]

        def slope(ref, dx):
            return ref[ob, dx + PADX, lo + 1 : hi + 1] - ref[ob, dx + PADX, lo - 1 : hi - 1]

        p[ob, PADX, lo:hi] = start[0]
        for step in range(STEPS):
            reach = 2 * step
            for dx in range(-reach, reach + 1):
                g[ob, dx + PADX, lo:hi] = bmw[ob, dx + inner] * at(p, dx)
            for dx in range(-reach - 1, reach + 2):
                if step == 0:
                    east, north = (start[1], start[2]) if dx == 0 else (None, None)
                elif abs(dx) <= reach - 2:
                    qv, sv = at(qp, dx), at(sp, dx)
                    east, north = qv - CORIOLIS * sv, sv + CORIOLIS * qv
                elif abs(dx) == reach - 1:
                    east = at(qp, dx)
                    north = CORIOLIS * east
                else:
                    east, north = None, None
                if abs(dx + 1) <= reach:
                    east = at(g, dx + 1) if east is None else east + at(g, dx + 1)
                if abs(dx - 1) <= reach:
                    east = -at(g, dx - 1) if east is None else east - at(g, dx - 1)
                qp[ob, dx + PADX, lo:hi] = east
                if abs(dx) <= reach:
                    rise = slope(g, dx)
                    north = rise if north is None else north + rise
                    if own_slot:
                        north = north * inside
                    sp[ob, dx + PADX, lo:hi] = north
            for dx in range(-reach - 2, reach + 3):
                change = None
                if abs(dx + 1) <= reach + 1:
                    change = at(qp, dx + 1)
                if abs(dx - 1) <= reach + 1:
                    change = -at(qp, dx - 1) if change is None else change - at(qp, dx - 1)
                if abs(dx) <= reach:
                    change = change + slope(sp, dx)
                change = A_COEF * change
                if abs(dx) <= reach:
                    change = change + at(p, dx)
                p[ob, dx + PADX, lo:hi] = change

    if own_slot:
        picked = slice(lo + rows // 2, lo + rows // 2 + rows)
    else:
        picked = pl.ds(pl.multiple_of(jnp.where(even, lo, lo + rows), SUB), rows)
    zero = jnp.zeros((rows, LANES), F32)
    blocks = nx // FINE
    shift = lax.rem(col + (nx - REACH), nx)
    depth_f = rows * nx
    total = None
    for f in range(3):
        for ob in range(nob):
            lane = slice(ob * LANES, (ob + 1) * LANES)
            fine = jnp.broadcast_to(lax.rem(shift[:, lane], FINE), (rows, LANES))
            bits = [(fine & (1 << i)) != 0 for i in range(4)]
            coarse = jnp.broadcast_to(shift[:, lane] // FINE, (FINE, LANES))
            marks = [(coarse == block).astype(F32).astype(BF16) for block in range(blocks)]
            values = [None] * (2 * FINE)
            for dx in range(-REACH, REACH + 1):
                if f == 0:
                    value = p[ob, dx + PADX, picked]
                elif abs(dx) <= REACH - 2:
                    qv, sv = qp[ob, dx + PADX, picked], sp[ob, dx + PADX, picked]
                    value = qv - CORIOLIS * sv if f == 1 else sv + CORIOLIS * qv
                elif abs(dx) == REACH - 1:
                    qv = qp[ob, dx + PADX, picked]
                    value = qv if f == 1 else CORIOLIS * qv
                else:
                    value = None
                values[dx + REACH] = value
            for i in range(4):
                moved = []
                for e in range(2 * FINE):
                    here = values[e]
                    there = values[e - (1 << i)] if e >= (1 << i) else None
                    if here is None and there is None:
                        moved.append(None)
                    else:
                        moved.append(
                            jnp.where(
                                bits[i],
                                zero if there is None else there,
                                zero if here is None else here,
                            )
                        )
                values = moved
            for e in range(2 * FINE):
                w[f, ob, e * rows : (e + 1) * rows, :] = zero if values[e] is None else values[e]
            for y in range(rows):
                both = halves(w[f, ob, pl.ds(y, 2 * FINE, stride=rows), :])
                for part, ref in zip(both, (sh, sl)):
                    near, far = part[:FINE], part[FINE:]
                    for block in range(blocks):
                        start_row = (f * rows + y) * nx + block * FINE
                        ref[start_row : start_row + FINE, lane] = (
                            near * marks[block] + far * marks[block - 1]
                        )
        span = slice(f * depth_f, (f + 1) * depth_f)
        basis = basis_ref[f]
        part = dot1(basis, sh[span, :]) + dot1(basis, sl[span, :])
        total = part if total is None else total + part
    out_ref[...] = total


def project(slot, own, first, second, basis, rows, nx):
    order = basis.shape[1]
    depth_all = 3 * rows * nx
    nobs = own.shape[1]
    nob = nobs // LANES
    wide = (nob, 2 * PADX + 1, 2 * rows + 2 * SUB, LANES)
    return pl.pallas_call(
        functools.partial(project_kernel, slot, rows, nx),
        out_shape=jax.ShapeDtypeStruct((order, nobs), F32),
        in_specs=[VMEM] * 4,
        out_specs=VMEM,
        scratch_shapes=[
            pltpu.VMEM((nob, 2 * REACH - 3, 2 * rows, LANES), F32),
            pltpu.VMEM(wide, F32),
            pltpu.VMEM(wide, F32),
            pltpu.VMEM(wide, F32),
            pltpu.VMEM(wide, F32),
            pltpu.VMEM((3, nob, 2 * FINE * rows, LANES), F32),
            pltpu.VMEM((depth_all, nobs), BF16),
            pltpu.VMEM((depth_all, nobs), BF16),
        ],
        compiler_params=params(48),
        cost_estimate=pl.CostEstimate(
            flops=4 * order * depth_all * nobs,
            bytes_accessed=2 * order * depth_all,
            transcendentals=0,
        ),
    )(own, first, second, basis)


def triangle_masks(half):
    rows = lax.broadcasted_iota(jnp.int32, (half, half), 0)
    cols = lax.broadcasted_iota(jnp.int32, (half, half), 1)
    return rows, cols


def store_packed(out_ref, matrix, vector):
    half = matrix.shape[0] // 2
    rows, cols = triangle_masks(half)
    corner = matrix[half:, half:]
    out_ref[0:half] = jnp.where(rows >= cols, matrix[:half, :half], corner)
    out_ref[half : 2 * half] = matrix[half:, :half]
    diagonal = jnp.sum(jnp.where(rows == cols, corner, 0.0), axis=0, keepdims=True)
    tail = jnp.concatenate(
        [vector[:, :half], vector[:, half:], diagonal, jnp.zeros((SUB - 3, half), F32)], axis=0
    )
    out_ref[2 * half : 2 * half + SUB] = tail


def load_packed(values):
    half = values.shape[1]
    rows, cols = triangle_masks(half)
    mixed = values[0:half]
    cross = values[half : 2 * half]
    vector = jnp.concatenate(
        [values[2 * half : 2 * half + 1], values[2 * half + 1 : 2 * half + 2]], axis=1
    )
    diagonal = values[2 * half + 2 : 2 * half + 3]
    turned = mixed.T
    first = jnp.where(rows >= cols, mixed, turned)
    last = jnp.where(rows == cols, diagonal, jnp.where(rows < cols, mixed, turned))
    top = jnp.concatenate([first, cross.T], axis=1)
    bottom = jnp.concatenate([cross, last], axis=1)
    return jnp.concatenate([top, bottom], axis=0), vector


def with_row(matrix, row):
    return jnp.concatenate([matrix, jnp.broadcast_to(row, (SUB, row.shape[1]))], axis=0)


def gram_kernel(own_ref, first_ref, second_ref, weight_ref, innovation_ref, out_ref):
    tile, tiles = lax.axis_index("tile"), lax.axis_size("tile")
    inner = (tile != 0) & (tile != tiles - 1)
    projected = own_ref[...] + first_ref[...] + jnp.where(inner, second_ref[...], 0.0)
    weight = weight_ref[...]
    left = with_row(projected * weight, weight * innovation_ref[...])
    result = dot3(halves(left), halves(projected), NT)
    size = projected.shape[0]
    store_packed(out_ref, result[:size], result[size : size + 1])


def gram(own, first, second, weight, innovation):
    order = own.shape[0]
    return pl.pallas_call(
        gram_kernel,
        out_shape=jax.ShapeDtypeStruct((order + SUB, order // 2), F32),
        in_specs=[VMEM] * 5,
        out_specs=VMEM,
        compiler_params=params(8),
        name="gram",
    )(own, first, second, weight, innovation)


def identity_like(matrix):
    rows = lax.broadcasted_iota(jnp.int32, matrix.shape, 0)
    cols = lax.broadcasted_iota(jnp.int32, matrix.shape, 1)
    return (rows == cols).astype(F32)


def norm_of(matrix):
    sums = jnp.sum(jnp.abs(matrix), axis=0, keepdims=True)
    return jnp.broadcast_to(jnp.max(sums, axis=1, keepdims=True), sums.shape)


def scaled(error):
    square = error * error
    rho = 2.0 / (2.0 - square)
    return rho, 0.5 * square * rho


def chebyshev_start(matrix, square, eye):
    bound = jnp.sqrt(norm_of(square))
    alpha = 2.0 / (2.0 + bound)
    error0 = 0.5 * bound * alpha
    rho, error = scaled(error0)
    rest = 1.0 - alpha
    factor = rho * alpha
    residual = rho * (
        (rest * rest) * eye - (2.0 * rest * alpha) * matrix + (alpha * alpha) * square
    ) - error * eye
    return factor * (2.0 - alpha), factor * alpha, residual, error, bound


def rough_turns(state, eye):
    size = eye.shape[0]
    new = []
    for estimate, residual, error in state:
        rho, error = scaled(error)
        part = residual.astype(BF16)
        moved = dot1(jnp.concatenate([estimate.astype(BF16), part], axis=0), part)
        new.append((rho * (estimate + moved[:size]), rho * moved[size:] - error * eye, error))
    return new


def polish(matrix, part, estimate, eye, exact):
    pieces = halves(estimate)
    moved = dot6(matrix, estimate) if exact else dot3(part, pieces)
    residual = eye - estimate - moved
    rough = residual.astype(BF16)
    change = residual + dot1(rough, rough)
    return estimate + dot3(pieces, halves(change))


def invert_any(matrix, part, c0, c1, error, eye):
    def unsure(state):
        return jnp.max(state[1]) > 0.03

    def turn(state):
        estimate, error = state
        pieces = halves(estimate)
        residual = 2.0 * eye - estimate - dot3(part, pieces)
        rho, error = scaled(error)
        return rho * dot3(pieces, halves(residual)), error

    estimate, error = lax.while_loop(unsure, turn, (c0 * eye - c1 * matrix, error))
    return lax.fori_loop(
        0, 4, lambda index, value: polish(matrix, part, value, eye, True), estimate
    )


def invert_shifted(matrices, parts, turns):
    eye = identity_like(matrices[0])
    state, starts, bounds = [], [], []
    for matrix, part in zip(matrices, parts):
        square = dot1(part[0], part[0])
        c0, c1, residual, error, bound = chebyshev_start(matrix, square, eye)
        state.append((c0 * eye - c1 * matrix, residual, error))
        starts.append((c0, c1, error))
        bounds.append(bound)
    narrow = jnp.max(functools.reduce(jnp.maximum, bounds)) < NARROW
    for _ in range(turns):
        state = rough_turns(state, eye)
    last = functools.reduce(jnp.maximum, [one[2] for one in state])
    enough = narrow & (jnp.max(last) < 0.04)
    quick = tuple(
        polish(m, part, one[0], eye, False) for m, part, one in zip(matrices, parts, state)
    )

    def careful():
        return tuple(
            invert_any(m, part, *start, eye) for m, part, start in zip(matrices, parts, starts)
        )

    return lax.cond(enough, lambda: quick, careful)


def solve_shifted(matrix, parts, row):
    eye = identity_like(matrix)
    row_parts = halves(row)
    extended = tuple(jnp.concatenate(two, axis=0) for two in zip(row_parts, parts))
    squares = dot3(extended, parts)
    moved, square = squares[:SUB], squares[SUB:]
    c0, c1, residual, error, _ = chebyshev_start(matrix, square, eye)
    rho, last = scaled(error)
    part = halves(residual)
    start = c0 * row - c1 * moved
    both = tuple(jnp.concatenate(two, axis=0) for two in zip(halves(start), part))
    moved = dot3(both, part)
    current = rho * (start + moved[:SUB])
    part = halves(rho * moved[SUB:] - last * eye)
    once = dot3(halves(current), part)
    quick = current + once + dot3(halves(once), part)

    def careful():
        inverse = invert_any(matrix, parts, c0, c1, error, eye)
        pieces = halves(inverse)

        def correct(index, value):
            miss = row - value - dot6(value, matrix)
            return value + dot3(halves(miss), pieces)

        return lax.fori_loop(0, 3, correct, dot3(row_parts, pieces))

    return lax.cond(jnp.max(last) < 0.03, lambda: quick, careful)


def column(row):
    size = row.shape[1]
    return jnp.broadcast_to(row, (size, size)).T


def row_dot(row, parts, dims=NN):
    return dot3(halves(jnp.broadcast_to(row, (SUB, row.shape[1]))), parts, dims)[0:1]


def pair_kernel(
    full, mine_ref, other_ref, transition_ref, model_error_ref,
    a_ref, j_ref, vec_ref, prefix_ref, *more,
):
    window = lax.axis_index("tm")
    lower_core = lax.rem(window, 2) == 0
    moves = jnp.where(window < 2, 0.0, 1.0)
    mine, other = mine_ref[...], other_ref[...]
    q2 = model_error_ref[...]
    size = q2.shape[1]
    root_row = jnp.sqrt(q2)
    root_col = column(root_row)
    transition = transition_ref[...]
    weighted = transition / column(q2)
    turned = halves(weighted.T)
    weighted = halves(weighted)
    mats, rows = [], []
    for packed in (jnp.where(lower_core, mine, other), jnp.where(lower_core, other, mine)):
        matrix, vector = load_packed(packed)
        mats.append(root_col * matrix * root_row)
        rows.append(root_row * vector)
    p1, p2 = invert_shifted(mats, [halves(m) for m in mats], 2)
    c1, c2 = root_col * p1 * root_row, root_col * p2 * root_row
    low = halves(c1)
    a2 = dot3(halves(c2), weighted)
    k1 = dot3(low, turned)
    rest2 = halves(transition - a2)
    crossed = dot3(halves(k1), rest2)
    a1 = moves * dot3(low, weighted)
    b1 = row_dot(rows[0], halves(p1)) * root_row
    b2 = row_dot(rows[1], halves(p2)) * root_row
    eta1 = moves * row_dot(b1, weighted)
    eta2 = row_dot(b2, weighted)
    j2 = dot3(turned, rest2)
    j1 = moves * dot3(turned, halves(transition - a1))
    a2_parts = halves(a2)
    a1_parts = halves(a1)
    j2_parts = halves(j2)
    outer = dot3(low, a2_parts, NT)
    ahead = row_dot(b1, a2_parts, NT) + b2
    behind = eta2 - row_dot(b1, j2_parts)
    spread = dot3(halves(a1.T), j2_parts)
    (inverse,) = invert_shifted([crossed], [halves(crossed)], 1)
    inverse = halves(inverse)
    both = tuple(
        jnp.concatenate(two, axis=1) for two in zip(a1_parts, halves(outer))
    )
    right = halves(dot3(inverse, both))
    s = row_dot(behind, inverse)
    ended = dot3(a2_parts, right)
    ended_rows = row_dot(s, both)
    trans, cov = ended[:, :size], ended[:, size:] + c2
    prec = dot3(halves(spread), tuple(part[:, :size] for part in right)) + j1
    info = ended_rows[:, :size] + eta1
    mean = ended_rows[:, size:] + ahead
    a_ref[...] = jnp.where(lower_core, a1, trans)
    j_ref[...] = jnp.where(lower_core, j1, prec)
    vec_ref[0:1] = jnp.where(lower_core, b1, mean)
    vec_ref[1:2] = jnp.where(lower_core, eta1, info)
    vec_ref[2:3] = mean
    vec_ref[3:4] = info
    vec_ref[4:SUB] = jnp.zeros((SUB - 4, size), F32)
    store_packed(prefix_ref, cov, mean)
    if full:
        for ref, value in zip(more, (trans, prec, cov)):
            ref[...] = value


def pair_up(mine, other, transition, model_error, full):
    order = transition.shape[0]
    square = jax.ShapeDtypeStruct((order, order), F32)
    shapes = [
        square,
        square,
        jax.ShapeDtypeStruct((SUB, order), F32),
        jax.ShapeDtypeStruct(mine.shape, F32),
    ] + [square] * (3 if full else 0)
    return pl.pallas_call(
        functools.partial(pair_kernel, full),
        out_shape=shapes,
        in_specs=[VMEM] * 4,
        out_specs=[VMEM] * len(shapes),
        compiler_params=params(24),
        name="pair_up",
    )(mine, other, transition, model_error)


def advance_kernel(incoming_ref, a_ref, j_ref, c_ref, vec_ref, out_ref):
    cov0, mean0 = load_packed(incoming_ref[...])
    low = halves(cov0)
    forward = halves(a_ref[...])
    back = halves(j_ref[...])
    crossed = dot3(low, back)
    outer = halves(dot3(low, forward, NT))
    behind = vec_ref[3:4] - row_dot(mean0, back)
    (inverse,) = invert_shifted([crossed], [halves(crossed)], 1)
    inverse = halves(inverse)
    s = row_dot(behind, inverse)
    mean = row_dot(mean0, forward, NT) + row_dot(s, outer) + vec_ref[2:3]
    cov = dot3(forward, halves(dot3(inverse, outer))) + c_ref[...]
    store_packed(out_ref, cov, mean)


def advance_prefix(incoming, a, j, c, vec):
    return pl.pallas_call(
        advance_kernel,
        out_shape=jax.ShapeDtypeStruct(incoming.shape, F32),
        in_specs=[VMEM] * 5,
        out_specs=VMEM,
        compiler_params=params(16),
        name="advance_prefix",
    )(incoming, a, j, c, vec)


def finish_kernel(rows, nx, incoming_ref, a_ref, j_ref, vec_ref, basis_ref, mean_ref, sum_ref):
    moves = jnp.where(lax.axis_index("tm") < 2, 0.0, 1.0)
    cov0, mean0 = load_packed(incoming_ref[...] * moves)
    size = mean0.shape[1]
    low = halves(with_row(cov0, mean0))
    crossed = dot3(low, halves(j_ref[...]))
    outer = dot3(low, halves(a_ref[...]), NT)
    matrix = crossed[:size]
    target = jnp.broadcast_to(vec_ref[1:2], (SUB, size)) - crossed[size:]
    s = solve_shifted(matrix, halves(matrix), target)
    mean = (dot3(halves(s), halves(outer[:size])) + outer[size:] + vec_ref[0:1])[0:1]
    mean_ref[...] = mean
    pieces = jnp.concatenate(list(thirds(mean)) + [jnp.zeros((5, size), BF16)], axis=0)
    for f in range(3):
        sums = dot1(pieces, basis_ref[f])
        total = sums[0:1] + (sums[1:2] + sums[2:3])
        for y in range(rows):
            i = f * rows + y
            sum_ref[i : i + 1, :] = total[:, y * nx : (y + 1) * nx]


def finish(incoming, a, j, vec, basis, rows, nx):
    order = a.shape[0]
    return pl.pallas_call(
        functools.partial(finish_kernel, rows, nx),
        out_shape=[
            jax.ShapeDtypeStruct((1, order), F32),
            jax.ShapeDtypeStruct((3 * rows, nx), F32),
        ],
        in_specs=[VMEM] * 5,
        out_specs=[VMEM] * 2,
        compiler_params=params(16),
        name="finish",
    )(incoming, a, j, vec, basis)


def increments_kernel(rows, nx, own_ref, first_ref, second_ref, mo, mf, ms, out_ref):
    tile, tiles = lax.axis_index("tile"), lax.axis_size("tile")

    def extend(own, first, second):
        before, after = before_after(first, second)
        return jnp.concatenate([before, own, after], axis=0)

    depth = extend(mo[0:rows, :], mf[0:rows, :], ms[0:rows, :]) * B_COEF
    h, u, v = [
        extend(*(ref[f * rows : (f + 1) * rows, :] for ref in (own_ref, first_ref, second_ref)))
        for f in range(3)
    ]
    total = 3 * rows
    y_iota = lax.broadcasted_iota(jnp.int32, (total, nx), 0)
    first_row = jnp.where(tile == 0, rows, 0)
    last_row = jnp.where(tile == tiles - 1, 2 * rows, total)
    inside = ((y_iota >= first_row) & (y_iota < last_row)).astype(F32)

    def diff_cols(values):
        return pltpu.roll(values, nx - 1, 1) - pltpu.roll(values, 1, 1)

    def diff_rows(values):
        return pltpu.roll(values, total - 1, 0) - pltpu.roll(values, 1, 0)

    for _ in range(STEPS):
        east = u + CORIOLIS * v - A_COEF * diff_cols(h)
        north = (v - CORIOLIS * u - A_COEF * diff_rows(h)) * inside
        h = h - depth * (diff_cols(east) + diff_rows(north))
        u, v = east, north
    for f, values in enumerate((h, u, v)):
        out_ref[f] = values[rows : 2 * rows]


def propagate_sum(own, first, second, mo, mf, ms, rows, nx):
    return pl.pallas_call(
        functools.partial(increments_kernel, rows, nx),
        out_shape=jax.ShapeDtypeStruct((3, rows, nx), F32),
        in_specs=[VMEM] * 6,
        out_specs=VMEM,
        compiler_params=params(8),
        name="propagate_sum",
    )(own, first, second, mo, mf, ms)


def layout_kernel(fields_ref, out_ref, held, sems, *spread):
    count, order, rows, nx = fields_ref.shape
    copies = [
        pltpu.make_async_copy(fields_ref.at[f], held.at[f], sems.at[f]) for f in range(count)
    ]
    for copy in copies:
        copy.start()
    for f, copy in enumerate(copies):
        copy.wait()
        for ob, ref in enumerate(spread):
            lane = slice(ob * LANES, (ob + 1) * LANES)
            ref[...] = held[f, :, :, lane].astype(F32).reshape(order * rows, LANES)
            for y in range(rows):
                start = y * nx + ob * LANES
                out_ref[f, :, start : start + LANES] = ref[
                    pl.ds(y, order, stride=rows), :
                ].astype(BF16)


def lay_out(fields):
    count, order, rows, nx = fields.shape
    return pl.pallas_call(
        layout_kernel,
        out_shape=jax.ShapeDtypeStruct((count, order, rows * nx), BF16),
        in_specs=[pl.BlockSpec(memory_space=pl.ANY)],
        out_specs=VMEM,
        scratch_shapes=[pltpu.VMEM(fields.shape, BF16), pltpu.SemaphoreType.DMA((count,))]
        + [pltpu.VMEM((order * rows, LANES), F32)] * (nx // LANES),
        compiler_params=params(50),
        name="lay_out",
    )(fields)


def info_kernel(depth_ref, cells_ref, fields_ref, out_ref, cells, fields, sems):
    rows = depth_ref.shape[0]
    copies = [
        pltpu.make_async_copy(source, target, sems.at[i])
        for i, (source, target) in enumerate((
            (depth_ref, out_ref.at[0:rows]), (cells_ref, cells), (fields_ref, fields),
        ))
    ]
    for copy in copies:
        copy.start()
    out_ref[rows : 2 * rows, :] = jnp.zeros(depth_ref.shape, F32)
    for copy in copies:
        copy.wait()
    out_ref[rows : rows + 1, :] = cells[...].astype(F32)
    out_ref[rows + 1 : rows + 2, :] = fields[...].astype(F32)


def gather_info(mean_depth, obs_cells, obs_fields):
    rows, nx = mean_depth.shape
    return pl.pallas_call(
        info_kernel,
        out_shape=jax.ShapeDtypeStruct((2 * rows, nx), F32),
        in_specs=[pl.BlockSpec(memory_space=pl.ANY)] * 3,
        out_specs=VMEM,
        scratch_shapes=[
            pltpu.VMEM(obs_cells.shape, jnp.int32),
            pltpu.VMEM(obs_fields.shape, jnp.int32),
            pltpu.SemaphoreType.DMA((3,)),
        ],
        compiler_params=params(60),
        name="gather_info",
    )(mean_depth, obs_cells, obs_fields)


def on_device(
    basis_fields, mean_depth, obs_cells, obs_fields, obs_weight, innovation, transition, model_error
):
    _, rows, nx = basis_fields.shape[2:]
    tiles = lax.axis_size("tile")
    windows = lax.axis_size("tm")
    near = [(i, i ^ 1) for i in range(tiles)]
    across = [i if i in (0, tiles - 1) else (i + 1 if i % 2 else i - 1) for i in range(tiles)]
    far = [
        (w * tiles + i, (w ^ 1 if across[i] == i else w) * tiles + across[i])
        for w in range(windows)
        for i in range(tiles)
    ]

    def swap_near(array):
        return lax.ppermute(array, "tile", near)

    def swap_far(array):
        return lax.ppermute(array, ("tm", "tile"), far)

    info = gather_info(mean_depth, obs_cells, obs_fields)
    info_near = swap_near(info)
    info_far = swap_far(info)
    basis = lay_out(basis_fields[0])

    part_near = project(NEAR, info, info_near, info_near, basis, rows, nx)
    got_near = swap_near(part_near)
    info_far, unused = lax.optimization_barrier((info_far, part_near))
    part_far = project(FAR, info, info_far, info_far, basis, rows, nx)
    got_far = swap_far(part_far)
    info_own, unused = lax.optimization_barrier((info, part_far))
    part_own = project(OWN, info_own, info_near, info_far, basis, rows, nx)

    packed = gram(part_own, got_near, got_far, obs_weight, innovation)
    bit = 1
    while bit < tiles:
        packed = packed + lax.ppermute(packed, "tile", [(i, i ^ bit) for i in range(tiles)])
        bit *= 2

    other = lax.ppermute(packed, "tm", [(i, i ^ 1) for i in range(windows)])
    pairs = windows // 2
    a, j, vec, prefix, *more = pair_up(
        packed, other, transition, model_error[None, :], pairs > 2
    )
    incoming = jnp.zeros_like(prefix)
    pair = lax.axis_index("tm") // 2
    for turn in range(pairs - 1):
        if pairs == 2:
            hop = [(i, i ^ 2) for i in range(windows)]
        else:
            hop = [(i, i + 2) for i in range(windows - 2)]
        incoming = lax.ppermute(prefix, "tm", hop)
        if turn < pairs - 2:
            longer = advance_prefix(incoming, *more, vec)
            prefix = jnp.where(pair == turn + 1, longer, prefix)
    mean, sums = finish(incoming, a, j, vec, basis, rows, nx)
    sums_near = swap_near(sums)
    sums_far = swap_far(sums)
    result = propagate_sum(sums, sums_near, sums_far, info, info_near, info_far, rows, nx)
    return mean, result[None]


def solution(mesh):
    return jax.shard_map(
        on_device,
        mesh=mesh,
        in_specs=(
            P("tm", None, None, "tile", None),
            P("tile", None),
            P("tm", "tile"),
            P("tm", "tile"),
            P("tm", "tile"),
            P("tm", "tile"),
            P(),
            P(),
        ),
        out_specs=(P("tm", None), P("tm", None, "tile", None)),
        check_vma=False,
    )
```

```python
import functools

import jax
import jax.numpy as jnp
from jax import lax
from jax.experimental import pallas as pl
from jax.experimental.pallas import tpu as pltpu
from jax.sharding import PartitionSpec as P


STEPS = 4
A_COEF = 0.5
B_COEF = 0.5
CORIOLIS = 0.3

F32 = jnp.float32
BF16 = jnp.bfloat16
LANES = 128
SUB = 8
REACH = 2 * STEPS
PADX = REACH + 1
NEAR, FAR, OWN = "project_near", "project_far", "project_own"
FINE = 16
NARROW = 16.0
HIGH = lax.Precision.HIGHEST
NT = (((1,), (1,)), ((), ()))
NN = (((1,), (0,)), ((), ()))
VMEM = pl.BlockSpec(memory_space=pltpu.VMEM)


def params(mib):
    return pltpu.CompilerParams(vmem_limit_bytes=mib << 20)


def dot6(left, right, dims=NN):
    return lax.dot_general(left, right, dims, precision=HIGH, preferred_element_type=F32)


def dot1(left, right, dims=NN):
    return lax.dot_general(left, right, dims, preferred_element_type=F32)


def halves(values):
    high = values.astype(BF16)
    return high, (values - high.astype(F32)).astype(BF16)


def thirds(values):
    high = values.astype(BF16)
    rest = values - high.astype(F32)
    mid = rest.astype(BF16)
    return high, mid, (rest - mid.astype(F32)).astype(BF16)


def dot3(left, right, dims=NN):
    (lh, ll), (rh, rl) = left, right
    return dot1(lh, rh, dims) + (dot1(lh, rl, dims) + dot1(ll, rh, dims))


def tile_dot(rows, parts, dims=NN):
    both = jnp.concatenate(halves(rows), axis=0)
    result = dot1(both, parts[0], dims) + dot1(both, parts[1], dims)
    return result[:SUB] + result[SUB:]


def row_dot(row, parts, dims=NN):
    return tile_dot(jnp.broadcast_to(row, (SUB, row.shape[1])), parts, dims)[0:1]


def before_after(first, second):
    tile, tiles = lax.axis_index("tile"), lax.axis_size("tile")
    even = lax.rem(tile, 2) == 0
    before = jnp.where(even, jnp.where(tile == 0, 0.0, second), first)
    after = jnp.where(even, first, jnp.where(tile == tiles - 1, 0.0, second))
    return before, after


def window_rows(slot, rows, even, own_ref, first_ref, second_ref):
    own = own_ref[0:rows, :] * B_COEF
    first = first_ref[0:rows, :] * B_COEF
    if slot == OWN:
        second = second_ref[0:rows, :] * B_COEF
        above, below = before_after(first, second)
        domain = jnp.concatenate([above[rows // 2 :], own, below[: rows // 2]], axis=0)
        base = rows // 2
    else:
        domain = jnp.concatenate(
            [jnp.where(even, own, first), jnp.where(even, first, own)], axis=0
        )
        base = jnp.where(even, rows, 0)
    return domain, base


def project_kernel(
    slot, rows, nx, own_ref, first_ref, second_ref, basis_ref, out_ref,
    bmw, p, g, qp, sp, w, sh, sl,
):
    own_slot = slot == OWN
    obs_ref = own_ref if own_slot else first_ref
    tile, tiles = lax.axis_index("tile"), lax.axis_size("tile")
    even = lax.rem(tile, 2) == (1 if slot == FAR else 0)
    domain, base = window_rows(slot, rows, even, own_ref, first_ref, second_ref)
    depth = 2 * rows
    nob = obs_ref.shape[1] // LANES
    inner = REACH - 2
    rolled = [
        pltpu.roll(domain, (-dx) % nx, 1) if dx else domain for dx in range(-inner, inner + 1)
    ]
    stacked = jnp.concatenate(rolled, axis=0)
    pieces = thirds(stacked)
    cells = obs_ref[rows : rows + 1, :]
    fields = obs_ref[rows + 1 : rows + 2, :]
    row_all = jnp.floor(cells * (1.0 / nx))
    col = (cells - row_all * nx).astype(jnp.int32)
    row = (row_all - rows * jnp.floor(row_all * (1.0 / rows))).astype(jnp.int32) + base
    field = fields.astype(jnp.int32)
    y_iota = lax.broadcasted_iota(jnp.int32, (depth, LANES), 0)
    x_iota = lax.broadcasted_iota(jnp.int32, (nx, LANES), 0)
    if own_slot:
        first_row = jnp.where(tile == 0, rows // 2, 0)
        last_row = jnp.where(tile == tiles - 1, rows // 2 + rows, depth)
        inside = ((y_iota >= first_row) & (y_iota < last_row)).astype(F32)
    lo, hi = SUB, SUB + depth
    zero_rows = jnp.zeros((SUB, LANES), F32)
    for ob in range(nob):
        lane = slice(ob * LANES, (ob + 1) * LANES)
        onehot = (x_iota == col[:, lane]).astype(F32).astype(BF16)
        depths = dot1(pieces[0], onehot) + (dot1(pieces[1], onehot) + dot1(pieces[2], onehot))
        for i in range(2 * inner + 1):
            bmw[ob, i] = depths[i * depth : (i + 1) * depth]
        for i in range(2 * PADX + 1):
            g[ob, i, 0:lo] = zero_rows
            g[ob, i, hi : hi + SUB] = zero_rows
            sp[ob, i, 0:lo] = zero_rows
            sp[ob, i, hi : hi + SUB] = zero_rows
        at_row = y_iota == row[:, lane]
        start = [(at_row & (field[:, lane] == f)).astype(F32) for f in range(3)]

        def at(ref, dx):
            return ref[ob, dx + PADX, lo:hi]

        def slope(ref, dx):
            return ref[ob, dx + PADX, lo + 1 : hi + 1] - ref[ob, dx + PADX, lo - 1 : hi - 1]

        p[ob, PADX, lo:hi] = start[0]
        for step in range(STEPS):
            reach = 2 * step
            for dx in range(-reach, reach + 1):
                g[ob, dx + PADX, lo:hi] = bmw[ob, dx + inner] * at(p, dx)
            for dx in range(-reach - 1, reach + 2):
                if step == 0:
                    east, north = (start[1], start[2]) if dx == 0 else (None, None)
                elif abs(dx) <= reach - 2:
                    qv, sv = at(qp, dx), at(sp, dx)
                    east, north = qv - CORIOLIS * sv, sv + CORIOLIS * qv
                elif abs(dx) == reach - 1:
                    east = at(qp, dx)
                    north = CORIOLIS * east
                else:
                    east, north = None, None
                if abs(dx + 1) <= reach:
                    east = at(g, dx + 1) if east is None else east + at(g, dx + 1)
                if abs(dx - 1) <= reach:
                    east = -at(g, dx - 1) if east is None else east - at(g, dx - 1)
                qp[ob, dx + PADX, lo:hi] = east
                if abs(dx) <= reach:
                    rise = slope(g, dx)
                    north = rise if north is None else north + rise
                    if own_slot:
                        north = north * inside
                    sp[ob, dx + PADX, lo:hi] = north
            for dx in range(-reach - 2, reach + 3):
                change = None
                if abs(dx + 1) <= reach + 1:
                    change = at(qp, dx + 1)
                if abs(dx - 1) <= reach + 1:
                    change = -at(qp, dx - 1) if change is None else change - at(qp, dx - 1)
                if abs(dx) <= reach:
                    change = change + slope(sp, dx)
                change = A_COEF * change
                if abs(dx) <= reach:
                    change = change + at(p, dx)
                p[ob, dx + PADX, lo:hi] = change

    if own_slot:
        picked = slice(lo + rows // 2, lo + rows // 2 + rows)
    else:
        picked = pl.ds(pl.multiple_of(jnp.where(even, lo, lo + rows), SUB), rows)
    zero = jnp.zeros((rows, LANES), F32)
    blocks = nx // FINE
    shift = lax.rem(col + (nx - REACH), nx)
    depth_f = rows * nx
    total = None
    for f in range(3):
        for ob in range(nob):
            lane = slice(ob * LANES, (ob + 1) * LANES)
            fine = jnp.broadcast_to(lax.rem(shift[:, lane], FINE), (rows, LANES))
            bits = [(fine & (1 << i)) != 0 for i in range(4)]
            coarse = jnp.broadcast_to(shift[:, lane] // FINE, (FINE, LANES))
            marks = [(coarse == block).astype(F32).astype(BF16) for block in range(blocks)]
            values = [None] * (2 * FINE)
            for dx in range(-REACH, REACH + 1):
                if f == 0:
                    value = p[ob, dx + PADX, picked]
                elif abs(dx) <= REACH - 2:
                    qv, sv = qp[ob, dx + PADX, picked], sp[ob, dx + PADX, picked]
                    value = qv - CORIOLIS * sv if f == 1 else sv + CORIOLIS * qv
                elif abs(dx) == REACH - 1:
                    qv = qp[ob, dx + PADX, picked]
                    value = qv if f == 1 else CORIOLIS * qv
                else:
                    value = None
                values[dx + REACH] = value
            for i in range(4):
                moved = []
                for e in range(2 * FINE):
                    here = values[e]
                    there = values[e - (1 << i)] if e >= (1 << i) else None
                    if here is None and there is None:
                        moved.append(None)
                    else:
                        moved.append(
                            jnp.where(
                                bits[i],
                                zero if there is None else there,
                                zero if here is None else here,
                            )
                        )
                values = moved
            for e in range(2 * FINE):
                w[f, ob, e * rows : (e + 1) * rows, :] = zero if values[e] is None else values[e]
            for y in range(rows):
                both = halves(w[f, ob, pl.ds(y, 2 * FINE, stride=rows), :])
                for part, ref in zip(both, (sh, sl)):
                    near, far = part[:FINE], part[FINE:]
                    for block in range(blocks):
                        start_row = (f * rows + y) * nx + block * FINE
                        ref[start_row : start_row + FINE, lane] = (
                            near * marks[block] + far * marks[block - 1]
                        )
        span = slice(f * depth_f, (f + 1) * depth_f)
        basis = basis_ref[f]
        part = dot1(basis, sh[span, :]) + dot1(basis, sl[span, :])
        total = part if total is None else total + part
    out_ref[...] = total


def project(slot, own, first, second, basis, rows, nx):
    order = basis.shape[1]
    depth_all = 3 * rows * nx
    nobs = own.shape[1]
    nob = nobs // LANES
    wide = (nob, 2 * PADX + 1, 2 * rows + 2 * SUB, LANES)
    return pl.pallas_call(
        functools.partial(project_kernel, slot, rows, nx),
        out_shape=jax.ShapeDtypeStruct((order, nobs), F32),
        in_specs=[VMEM] * 4,
        out_specs=VMEM,
        scratch_shapes=[
            pltpu.VMEM((nob, 2 * REACH - 3, 2 * rows, LANES), F32),
            pltpu.VMEM(wide, F32),
            pltpu.VMEM(wide, F32),
            pltpu.VMEM(wide, F32),
            pltpu.VMEM(wide, F32),
            pltpu.VMEM((3, nob, 2 * FINE * rows, LANES), F32),
            pltpu.VMEM((depth_all, nobs), BF16),
            pltpu.VMEM((depth_all, nobs), BF16),
        ],
        compiler_params=params(48),
        cost_estimate=pl.CostEstimate(
            flops=4 * order * depth_all * nobs,
            bytes_accessed=2 * order * depth_all,
            transcendentals=0,
        ),
    )(own, first, second, basis)


def triangle_masks(half):
    rows = lax.broadcasted_iota(jnp.int32, (half, half), 0)
    cols = lax.broadcasted_iota(jnp.int32, (half, half), 1)
    return rows, cols


def store_packed(out_ref, matrix, vector):
    half = matrix.shape[0] // 2
    rows, cols = triangle_masks(half)
    corner = matrix[half:, half:]
    out_ref[0:half] = jnp.where(rows >= cols, matrix[:half, :half], corner)
    out_ref[half : 2 * half] = matrix[half:, :half]
    diagonal = jnp.sum(jnp.where(rows == cols, corner, 0.0), axis=0, keepdims=True)
    tail = jnp.concatenate(
        [vector[:, :half], vector[:, half:], diagonal, jnp.zeros((SUB - 3, half), F32)], axis=0
    )
    out_ref[2 * half : 2 * half + SUB] = tail


def load_packed(values):
    half = values.shape[1]
    rows, cols = triangle_masks(half)
    mixed = values[0:half]
    cross = values[half : 2 * half]
    vector = jnp.concatenate(
        [values[2 * half : 2 * half + 1], values[2 * half + 1 : 2 * half + 2]], axis=1
    )
    diagonal = values[2 * half + 2 : 2 * half + 3]
    turned = mixed.T
    first = jnp.where(rows >= cols, mixed, turned)
    last = jnp.where(rows == cols, diagonal, jnp.where(rows < cols, mixed, turned))
    top = jnp.concatenate([first, cross.T], axis=1)
    bottom = jnp.concatenate([cross, last], axis=1)
    return jnp.concatenate([top, bottom], axis=0), vector


def with_row(matrix, row):
    return jnp.concatenate([matrix, jnp.broadcast_to(row, (SUB, row.shape[1]))], axis=0)


def gram_kernel(own_ref, first_ref, second_ref, weight_ref, innovation_ref, out_ref):
    tile, tiles = lax.axis_index("tile"), lax.axis_size("tile")
    inner = (tile != 0) & (tile != tiles - 1)
    projected = own_ref[...] + first_ref[...] + jnp.where(inner, second_ref[...], 0.0)
    weight = weight_ref[...]
    left = with_row(projected * weight, weight * innovation_ref[...])
    result = dot3(halves(left), halves(projected), NT)
    size = projected.shape[0]
    store_packed(out_ref, result[:size], result[size : size + 1])


def gram(own, first, second, weight, innovation):
    order = own.shape[0]
    return pl.pallas_call(
        gram_kernel,
        out_shape=jax.ShapeDtypeStruct((order + SUB, order // 2), F32),
        in_specs=[VMEM] * 5,
        out_specs=VMEM,
        compiler_params=params(8),
        name="gram",
    )(own, first, second, weight, innovation)


def identity_like(matrix):
    rows = lax.broadcasted_iota(jnp.int32, matrix.shape, 0)
    cols = lax.broadcasted_iota(jnp.int32, matrix.shape, 1)
    return (rows == cols).astype(F32)


def norm_of(matrix):
    sums = jnp.sum(jnp.abs(matrix), axis=0, keepdims=True)
    return jnp.broadcast_to(jnp.max(sums, axis=1, keepdims=True), sums.shape)


def scaled(error):
    square = error * error
    rho = 2.0 / (2.0 - square)
    return rho, 0.5 * square * rho


def chebyshev_start(matrix, square, eye):
    bound = jnp.sqrt(norm_of(square))
    alpha = 2.0 / (2.0 + bound)
    error0 = 0.5 * bound * alpha
    rho, error = scaled(error0)
    rest = 1.0 - alpha
    factor = rho * alpha
    residual = rho * (
        (rest * rest) * eye - (2.0 * rest * alpha) * matrix + (alpha * alpha) * square
    ) - error * eye
    return factor * (2.0 - alpha), factor * alpha, residual, error, bound


def rough_turns(state, eye):
    size = eye.shape[0]
    new = []
    for estimate, residual, error in state:
        rho, error = scaled(error)
        part = residual.astype(BF16)
        moved = dot1(jnp.concatenate([estimate.astype(BF16), part], axis=0), part)
        new.append((rho * (estimate + moved[:size]), rho * moved[size:] - error * eye, error))
    return new


def polish(matrix, part, estimate, eye, exact):
    pieces = halves(estimate)
    moved = dot6(matrix, estimate) if exact else dot3(part, pieces)
    residual = eye - estimate - moved
    rough = residual.astype(BF16)
    change = residual + dot1(rough, rough)
    return estimate + dot3(pieces, halves(change))


def invert_any(matrix, part, c0, c1, error, eye):
    def unsure(state):
        return jnp.max(state[1]) > 0.03

    def turn(state):
        estimate, error = state
        pieces = halves(estimate)
        residual = 2.0 * eye - estimate - dot3(part, pieces)
        rho, error = scaled(error)
        return rho * dot3(pieces, halves(residual)), error

    estimate, error = lax.while_loop(unsure, turn, (c0 * eye - c1 * matrix, error))
    return lax.fori_loop(
        0, 4, lambda index, value: polish(matrix, part, value, eye, True), estimate
    )


def invert_shifted(matrices, parts, turns):
    eye = identity_like(matrices[0])
    state, starts, bounds = [], [], []
    for matrix, part in zip(matrices, parts):
        square = dot1(part[0], part[0])
        c0, c1, residual, error, bound = chebyshev_start(matrix, square, eye)
        state.append((c0 * eye - c1 * matrix, residual, error))
        starts.append((c0, c1, error))
        bounds.append(bound)
    narrow = jnp.max(functools.reduce(jnp.maximum, bounds)) < NARROW
    for _ in range(turns):
        state = rough_turns(state, eye)
    last = functools.reduce(jnp.maximum, [one[2] for one in state])
    enough = narrow & (jnp.max(last) < 0.04)
    quick = tuple(
        polish(m, part, one[0], eye, False) for m, part, one in zip(matrices, parts, state)
    )

    def careful():
        return tuple(
            invert_any(m, part, *start, eye) for m, part, start in zip(matrices, parts, starts)
        )

    return lax.cond(enough, lambda: quick, careful)


def solve_shifted(matrix, parts, row):
    eye = identity_like(matrix)
    row_parts = halves(row)
    extended = tuple(jnp.concatenate(two, axis=0) for two in zip(row_parts, parts))
    squares = dot3(extended, parts)
    moved, square = squares[:SUB], squares[SUB:]
    c0, c1, residual, error, _ = chebyshev_start(matrix, square, eye)
    rho, last = scaled(error)
    part = halves(residual)
    start = c0 * row - c1 * moved
    both = tuple(jnp.concatenate(two, axis=0) for two in zip(halves(start), part))
    moved = dot3(both, part)
    current = rho * (start + moved[:SUB])
    part = halves(rho * moved[SUB:] - last * eye)
    once = tile_dot(current, part)
    quick = current + once + tile_dot(once, part)

    def careful():
        inverse = invert_any(matrix, parts, c0, c1, error, eye)
        pieces = halves(inverse)

        def correct(index, value):
            miss = row - value - dot6(value, matrix)
            return value + dot3(halves(miss), pieces)

        return lax.fori_loop(0, 3, correct, dot3(row_parts, pieces))

    return lax.cond(jnp.max(last) < 0.03, lambda: quick, careful)


def column(row):
    size = row.shape[1]
    return jnp.broadcast_to(row, (size, size)).T


def pair_kernel(
    full, mine_ref, other_ref, transition_ref, model_error_ref,
    a_ref, j_ref, vec_ref, prefix_ref, *more,
):
    window = lax.axis_index("tm")
    lower_core = lax.rem(window, 2) == 0
    moves = jnp.where(window < 2, 0.0, 1.0)
    mine, other = mine_ref[...], other_ref[...]
    q2 = model_error_ref[...]
    size = q2.shape[1]
    root_row = jnp.sqrt(q2)
    root_col = column(root_row)
    transition = transition_ref[...]
    weighted = transition / column(q2)
    turned = halves(weighted.T)
    weighted = halves(weighted)
    mats, rows = [], []
    for packed in (jnp.where(lower_core, mine, other), jnp.where(lower_core, other, mine)):
        matrix, vector = load_packed(packed)
        mats.append(root_col * matrix * root_row)
        rows.append(root_row * vector)
    p1, p2 = invert_shifted(mats, [halves(m) for m in mats], 2)
    c1, c2 = root_col * p1 * root_row, root_col * p2 * root_row
    low = halves(c1)
    a2 = dot3(halves(c2), weighted)
    k1 = dot3(low, turned)
    rest2 = halves(transition - a2)
    crossed = dot3(halves(k1), rest2)
    a1 = moves * dot3(low, weighted)
    b1 = row_dot(rows[0], halves(p1)) * root_row
    b2 = row_dot(rows[1], halves(p2)) * root_row
    eta1 = moves * row_dot(b1, weighted)
    eta2 = row_dot(b2, weighted)
    j2 = dot3(turned, rest2)
    j1 = moves * dot3(turned, halves(transition - a1))
    a2_parts = halves(a2)
    a1_parts = halves(a1)
    j2_parts = halves(j2)
    outer = dot3(low, a2_parts, NT)
    ahead = row_dot(b1, a2_parts, NT) + b2
    behind = eta2 - row_dot(b1, j2_parts)
    spread = dot3(halves(a1.T), j2_parts)
    (inverse,) = invert_shifted([crossed], [halves(crossed)], 1)
    inverse = halves(inverse)
    both = tuple(
        jnp.concatenate(two, axis=1) for two in zip(a1_parts, halves(outer))
    )
    right = halves(dot3(inverse, both))
    s = row_dot(behind, inverse)
    ended = dot3(a2_parts, right)
    ended_rows = row_dot(s, both)
    trans, cov = ended[:, :size], ended[:, size:] + c2
    prec = dot3(halves(spread), tuple(part[:, :size] for part in right)) + j1
    info = ended_rows[:, :size] + eta1
    mean = ended_rows[:, size:] + ahead
    a_ref[...] = jnp.where(lower_core, a1, trans)
    j_ref[...] = jnp.where(lower_core, j1, prec)
    vec_ref[0:1] = jnp.where(lower_core, b1, mean)
    vec_ref[1:2] = jnp.where(lower_core, eta1, info)
    vec_ref[2:3] = mean
    vec_ref[3:4] = info
    vec_ref[4:SUB] = jnp.zeros((SUB - 4, size), F32)
    store_packed(prefix_ref, cov, mean)
    if full:
        for ref, value in zip(more, (trans, prec, cov)):
            ref[...] = value


def pair_up(mine, other, transition, model_error, full):
    order = transition.shape[0]
    square = jax.ShapeDtypeStruct((order, order), F32)
    shapes = [
        square,
        square,
        jax.ShapeDtypeStruct((SUB, order), F32),
        jax.ShapeDtypeStruct(mine.shape, F32),
    ] + [square] * (3 if full else 0)
    return pl.pallas_call(
        functools.partial(pair_kernel, full),
        out_shape=shapes,
        in_specs=[VMEM] * 4,
        out_specs=[VMEM] * len(shapes),
        compiler_params=params(24),
        name="pair_up",
    )(mine, other, transition, model_error)


def advance_kernel(incoming_ref, a_ref, j_ref, c_ref, vec_ref, out_ref):
    cov0, mean0 = load_packed(incoming_ref[...])
    low = halves(cov0)
    forward = halves(a_ref[...])
    back = halves(j_ref[...])
    crossed = dot3(low, back)
    outer = halves(dot3(low, forward, NT))
    behind = vec_ref[3:4] - row_dot(mean0, back)
    (inverse,) = invert_shifted([crossed], [halves(crossed)], 1)
    inverse = halves(inverse)
    s = row_dot(behind, inverse)
    mean = row_dot(mean0, forward, NT) + row_dot(s, outer) + vec_ref[2:3]
    cov = dot3(forward, halves(dot3(inverse, outer))) + c_ref[...]
    store_packed(out_ref, cov, mean)


def advance_prefix(incoming, a, j, c, vec):
    return pl.pallas_call(
        advance_kernel,
        out_shape=jax.ShapeDtypeStruct(incoming.shape, F32),
        in_specs=[VMEM] * 5,
        out_specs=VMEM,
        compiler_params=params(16),
        name="advance_prefix",
    )(incoming, a, j, c, vec)


def finish_kernel(rows, nx, incoming_ref, a_ref, j_ref, vec_ref, basis_ref, mean_ref, sum_ref):
    moves = jnp.where(lax.axis_index("tm") < 2, 0.0, 1.0)
    cov0, mean0 = load_packed(incoming_ref[...] * moves)
    size = mean0.shape[1]
    low = halves(with_row(cov0, mean0))
    crossed = dot3(low, halves(j_ref[...]))
    outer = dot3(low, halves(a_ref[...]), NT)
    matrix = crossed[:size]
    target = jnp.broadcast_to(vec_ref[1:2], (SUB, size)) - crossed[size:]
    s = solve_shifted(matrix, halves(matrix), target)
    mean = (tile_dot(s, halves(outer[:size])) + outer[size:] + vec_ref[0:1])[0:1]
    mean_ref[...] = mean
    pieces = jnp.concatenate(list(thirds(mean)) + [jnp.zeros((5, size), BF16)], axis=0)
    for f in range(3):
        sums = dot1(pieces, basis_ref[f])
        total = sums[0:1] + (sums[1:2] + sums[2:3])
        for y in range(rows):
            i = f * rows + y
            sum_ref[i : i + 1, :] = total[:, y * nx : (y + 1) * nx]


def finish(incoming, a, j, vec, basis, rows, nx):
    order = a.shape[0]
    return pl.pallas_call(
        functools.partial(finish_kernel, rows, nx),
        out_shape=[
            jax.ShapeDtypeStruct((1, order), F32),
            jax.ShapeDtypeStruct((3 * rows, nx), F32),
        ],
        in_specs=[VMEM] * 5,
        out_specs=[VMEM] * 2,
        compiler_params=params(16),
        name="finish",
    )(incoming, a, j, vec, basis)


def increments_kernel(rows, nx, own_ref, first_ref, second_ref, mo, mf, ms, out_ref):
    tile, tiles = lax.axis_index("tile"), lax.axis_size("tile")

    def extend(own, first, second):
        before, after = before_after(first, second)
        return jnp.concatenate([before, own, after], axis=0)

    depth = extend(mo[0:rows, :], mf[0:rows, :], ms[0:rows, :]) * B_COEF
    h, u, v = [
        extend(*(ref[f * rows : (f + 1) * rows, :] for ref in (own_ref, first_ref, second_ref)))
        for f in range(3)
    ]
    total = 3 * rows
    y_iota = lax.broadcasted_iota(jnp.int32, (total, nx), 0)
    first_row = jnp.where(tile == 0, rows, 0)
    last_row = jnp.where(tile == tiles - 1, 2 * rows, total)
    inside = ((y_iota >= first_row) & (y_iota < last_row)).astype(F32)

    def cols(values, by):
        return pltpu.roll(values, by % nx, 1)

    def lines(values, by):
        return pltpu.roll(values, by % total, 0)

    after, before = lines(inside, -1), lines(inside, 1)
    for _ in range(STEPS):
        east, north = u + CORIOLIS * v, v - CORIOLIS * u
        slope_cols = cols(east, -1) - cols(east, 1) - A_COEF * (
            (cols(h, -2) - h) - (h - cols(h, 2))
        )
        slope_lines = after * (lines(north, -1) - A_COEF * (lines(h, -2) - h)) - before * (
            lines(north, 1) - A_COEF * (h - lines(h, 2))
        )
        u = east - A_COEF * (cols(h, -1) - cols(h, 1))
        v = inside * (north - A_COEF * (lines(h, -1) - lines(h, 1)))
        h = h - depth * (slope_cols + slope_lines)
    for f, values in enumerate((h, u, v)):
        out_ref[f] = values[rows : 2 * rows]


def propagate_sum(own, first, second, mo, mf, ms, rows, nx):
    return pl.pallas_call(
        functools.partial(increments_kernel, rows, nx),
        out_shape=jax.ShapeDtypeStruct((3, rows, nx), F32),
        in_specs=[VMEM] * 6,
        out_specs=VMEM,
        compiler_params=params(8),
        name="propagate_sum",
    )(own, first, second, mo, mf, ms)


def layout_kernel(fields_ref, out_ref, held, sems, *spread):
    count, order, rows, nx = fields_ref.shape
    copies = [
        pltpu.make_async_copy(fields_ref.at[f], held.at[f], sems.at[f]) for f in range(count)
    ]
    for copy in copies:
        copy.start()
    for f, copy in enumerate(copies):
        copy.wait()
        for ob, ref in enumerate(spread):
            lane = slice(ob * LANES, (ob + 1) * LANES)
            ref[...] = held[f, :, :, lane].astype(F32).reshape(order * rows, LANES)
            for y in range(rows):
                start = y * nx + ob * LANES
                out_ref[f, :, start : start + LANES] = ref[
                    pl.ds(y, order, stride=rows), :
                ].astype(BF16)


def lay_out(fields):
    count, order, rows, nx = fields.shape
    return pl.pallas_call(
        layout_kernel,
        out_shape=jax.ShapeDtypeStruct((count, order, rows * nx), BF16),
        in_specs=[pl.BlockSpec(memory_space=pl.ANY)],
        out_specs=VMEM,
        scratch_shapes=[pltpu.VMEM(fields.shape, BF16), pltpu.SemaphoreType.DMA((count,))]
        + [pltpu.VMEM((order * rows, LANES), F32)] * (nx // LANES),
        compiler_params=params(50),
        name="lay_out",
    )(fields)


def info_kernel(depth_ref, cells_ref, fields_ref, out_ref, cells, fields, sems):
    rows = depth_ref.shape[0]
    copies = [
        pltpu.make_async_copy(source, target, sems.at[i])
        for i, (source, target) in enumerate((
            (depth_ref, out_ref.at[0:rows]), (cells_ref, cells), (fields_ref, fields),
        ))
    ]
    for copy in copies:
        copy.start()
    out_ref[rows : 2 * rows, :] = jnp.zeros(depth_ref.shape, F32)
    for copy in copies:
        copy.wait()
    out_ref[rows : rows + 1, :] = cells[...].astype(F32)
    out_ref[rows + 1 : rows + 2, :] = fields[...].astype(F32)


def gather_info(mean_depth, obs_cells, obs_fields):
    rows, nx = mean_depth.shape
    return pl.pallas_call(
        info_kernel,
        out_shape=jax.ShapeDtypeStruct((2 * rows, nx), F32),
        in_specs=[pl.BlockSpec(memory_space=pl.ANY)] * 3,
        out_specs=VMEM,
        scratch_shapes=[
            pltpu.VMEM(obs_cells.shape, jnp.int32),
            pltpu.VMEM(obs_fields.shape, jnp.int32),
            pltpu.SemaphoreType.DMA((3,)),
        ],
        compiler_params=params(60),
        name="gather_info",
    )(mean_depth, obs_cells, obs_fields)


def on_device(
    basis_fields, mean_depth, obs_cells, obs_fields, obs_weight, innovation, transition, model_error
):
    _, rows, nx = basis_fields.shape[2:]
    tiles = lax.axis_size("tile")
    windows = lax.axis_size("tm")
    near = [(i, i ^ 1) for i in range(tiles)]
    across = [i if i in (0, tiles - 1) else (i + 1 if i % 2 else i - 1) for i in range(tiles)]
    far = [
        (w * tiles + i, (w ^ 1 if across[i] == i else w) * tiles + across[i])
        for w in range(windows)
        for i in range(tiles)
    ]

    def swap_near(array):
        return lax.ppermute(array, "tile", near)

    def swap_far(array):
        return lax.ppermute(array, ("tm", "tile"), far)

    info = gather_info(mean_depth, obs_cells, obs_fields)
    info_near = swap_near(info)
    info_far = swap_far(info)
    basis = lay_out(basis_fields[0])

    part_near = project(NEAR, info, info_near, info_near, basis, rows, nx)
    got_near = swap_near(part_near)
    info_far, unused = lax.optimization_barrier((info_far, part_near))
    part_far = project(FAR, info, info_far, info_far, basis, rows, nx)
    got_far = swap_far(part_far)
    info_own, unused = lax.optimization_barrier((info, part_far))
    part_own = project(OWN, info_own, info_near, info_far, basis, rows, nx)

    packed = gram(part_own, got_near, got_far, obs_weight, innovation)
    bit = 1
    while bit < tiles:
        reach = 3 if bit * 2 < tiles else 1
        parts = [
            lax.ppermute(packed, "tile", [(i, i ^ (bit * by)) for i in range(tiles)])
            for by in range(1, reach + 1)
        ]
        packed = packed + parts[0]
        if reach == 3:
            packed = packed + (parts[1] + parts[2])
        bit *= reach + 1
    other = lax.ppermute(packed, "tm", [(i, i ^ 1) for i in range(windows)])
    pairs = windows // 2
    a, j, vec, prefix, *more = pair_up(
        packed, other, transition, model_error[None, :], pairs > 2
    )
    incoming = jnp.zeros_like(prefix)
    pair = lax.axis_index("tm") // 2
    for turn in range(pairs - 1):
        if pairs == 2:
            hop = [(i, i ^ 2) for i in range(windows)]
        else:
            hop = [(i, i + 2) for i in range(windows - 2)]
        incoming = lax.ppermute(prefix, "tm", hop)
        if turn < pairs - 2:
            longer = advance_prefix(incoming, *more, vec)
            prefix = jnp.where(pair == turn + 1, longer, prefix)
    mean, sums = finish(incoming, a, j, vec, basis, rows, nx)
    sums_near = swap_near(sums)
    sums_far = swap_far(sums)
    result = propagate_sum(sums, sums_near, sums_far, info, info_near, info_far, rows, nx)
    return mean, result[None]


def solution(mesh):
    return jax.shard_map(
        on_device,
        mesh=mesh,
        in_specs=(
            P("tm", None, None, "tile", None),
            P("tile", None),
            P("tm", "tile"),
            P("tm", "tile"),
            P("tm", "tile"),
            P("tm", "tile"),
            P(),
            P(),
        ),
        out_specs=(P("tm", None), P("tm", None, "tile", None)),
        check_vma=False,
    )
```

```python
import functools

import jax
import jax.numpy as jnp
from jax import lax
from jax.experimental import pallas as pl
from jax.experimental.pallas import tpu as pltpu
from jax.sharding import PartitionSpec as P


STEPS = 4
A_COEF = 0.5
B_COEF = 0.5
CORIOLIS = 0.3

F32 = jnp.float32
BF16 = jnp.bfloat16
LANES = 128
SUB = 8
REACH = 2 * STEPS
PADX = REACH + 1
NEAR, FAR, OWN = "project_near", "project_far", "project_own"
FINE = 16
NARROW = 16.0
HIGH = lax.Precision.HIGHEST
NT = (((1,), (1,)), ((), ()))
NN = (((1,), (0,)), ((), ()))
VMEM = pl.BlockSpec(memory_space=pltpu.VMEM)


def params(mib):
    return pltpu.CompilerParams(vmem_limit_bytes=mib << 20)


def dot6(left, right, dims=NN):
    return lax.dot_general(left, right, dims, precision=HIGH, preferred_element_type=F32)


def dot1(left, right, dims=NN):
    return lax.dot_general(left, right, dims, preferred_element_type=F32)


def halves(values):
    high = values.astype(BF16)
    return high, (values - high.astype(F32)).astype(BF16)


def thirds(values):
    high = values.astype(BF16)
    rest = values - high.astype(F32)
    mid = rest.astype(BF16)
    return high, mid, (rest - mid.astype(F32)).astype(BF16)


def dot3(left, right, dims=NN):
    (lh, ll), (rh, rl) = left, right
    return dot1(lh, rh, dims) + (dot1(lh, rl, dims) + dot1(ll, rh, dims))


def tile_dot(rows, parts, dims=NN):
    both = jnp.concatenate(halves(rows), axis=0)
    result = dot1(both, parts[0], dims) + dot1(both, parts[1], dims)
    return result[:SUB] + result[SUB:]


def row_dot(row, parts, dims=NN):
    return tile_dot(jnp.broadcast_to(row, (SUB, row.shape[1])), parts, dims)[0:1]


def before_after(first, second):
    tile, tiles = lax.axis_index("tile"), lax.axis_size("tile")
    even = lax.rem(tile, 2) == 0
    before = jnp.where(even, jnp.where(tile == 0, 0.0, second), first)
    after = jnp.where(even, first, jnp.where(tile == tiles - 1, 0.0, second))
    return before, after


def window_rows(slot, rows, even, own_ref, first_ref, second_ref):
    own = own_ref[0:rows, :] * B_COEF
    first = first_ref[0:rows, :] * B_COEF
    if slot == OWN:
        second = second_ref[0:rows, :] * B_COEF
        above, below = before_after(first, second)
        domain = jnp.concatenate([above[rows // 2 :], own, below[: rows // 2]], axis=0)
        base = rows // 2
    else:
        domain = jnp.concatenate(
            [jnp.where(even, own, first), jnp.where(even, first, own)], axis=0
        )
        base = jnp.where(even, rows, 0)
    return domain, base


def project_kernel(
    slot, rows, nx, own_ref, first_ref, second_ref, basis_ref, out_ref,
    bmw, p, g, qp, sp, w, sh, sl,
):
    own_slot = slot == OWN
    obs_ref = own_ref if own_slot else first_ref
    tile, tiles = lax.axis_index("tile"), lax.axis_size("tile")
    even = lax.rem(tile, 2) == (1 if slot == FAR else 0)
    domain, base = window_rows(slot, rows, even, own_ref, first_ref, second_ref)
    depth = 2 * rows
    nob = obs_ref.shape[1] // LANES
    inner = REACH - 2
    rolled = [
        pltpu.roll(domain, (-dx) % nx, 1) if dx else domain for dx in range(-inner, inner + 1)
    ]
    stacked = jnp.concatenate(rolled, axis=0)
    pieces = thirds(stacked)
    cells = obs_ref[rows : rows + 1, :]
    fields = obs_ref[rows + 1 : rows + 2, :]
    row_all = jnp.floor(cells * (1.0 / nx))
    col = (cells - row_all * nx).astype(jnp.int32)
    row = (row_all - rows * jnp.floor(row_all * (1.0 / rows))).astype(jnp.int32) + base
    field = fields.astype(jnp.int32)
    y_iota = lax.broadcasted_iota(jnp.int32, (depth, LANES), 0)
    x_iota = lax.broadcasted_iota(jnp.int32, (nx, LANES), 0)
    if own_slot:
        first_row = jnp.where(tile == 0, rows // 2, 0)
        last_row = jnp.where(tile == tiles - 1, rows // 2 + rows, depth)
        inside = ((y_iota >= first_row) & (y_iota < last_row)).astype(F32)
    lo, hi = SUB, SUB + depth
    zero_rows = jnp.zeros((SUB, LANES), F32)
    for ob in range(nob):
        lane = slice(ob * LANES, (ob + 1) * LANES)
        onehot = (x_iota == col[:, lane]).astype(F32).astype(BF16)
        depths = dot1(pieces[0], onehot) + (dot1(pieces[1], onehot) + dot1(pieces[2], onehot))
        for i in range(2 * inner + 1):
            bmw[ob, i] = depths[i * depth : (i + 1) * depth]
        for i in range(2 * PADX + 1):
            g[ob, i, 0:lo] = zero_rows
            g[ob, i, hi : hi + SUB] = zero_rows
            sp[ob, i, 0:lo] = zero_rows
            sp[ob, i, hi : hi + SUB] = zero_rows
        at_row = y_iota == row[:, lane]
        start = [(at_row & (field[:, lane] == f)).astype(F32) for f in range(3)]

        def at(ref, dx):
            return ref[ob, dx + PADX, lo:hi]

        def slope(ref, dx):
            return ref[ob, dx + PADX, lo + 1 : hi + 1] - ref[ob, dx + PADX, lo - 1 : hi - 1]

        p[ob, PADX, lo:hi] = start[0]
        for step in range(STEPS):
            reach = 2 * step
            for dx in range(-reach, reach + 1):
                g[ob, dx + PADX, lo:hi] = bmw[ob, dx + inner] * at(p, dx)
            for dx in range(-reach - 1, reach + 2):
                if step == 0:
                    east, north = (start[1], start[2]) if dx == 0 else (None, None)
                elif abs(dx) <= reach - 2:
                    qv, sv = at(qp, dx), at(sp, dx)
                    east, north = qv - CORIOLIS * sv, sv + CORIOLIS * qv
                elif abs(dx) == reach - 1:
                    east = at(qp, dx)
                    north = CORIOLIS * east
                else:
                    east, north = None, None
                if abs(dx + 1) <= reach:
                    east = at(g, dx + 1) if east is None else east + at(g, dx + 1)
                if abs(dx - 1) <= reach:
                    east = -at(g, dx - 1) if east is None else east - at(g, dx - 1)
                qp[ob, dx + PADX, lo:hi] = east
                if abs(dx) <= reach:
                    rise = slope(g, dx)
                    north = rise if north is None else north + rise
                    if own_slot:
                        north = north * inside
                    sp[ob, dx + PADX, lo:hi] = north
            for dx in range(-reach - 2, reach + 3):
                change = None
                if abs(dx + 1) <= reach + 1:
                    change = at(qp, dx + 1)
                if abs(dx - 1) <= reach + 1:
                    change = -at(qp, dx - 1) if change is None else change - at(qp, dx - 1)
                if abs(dx) <= reach:
                    change = change + slope(sp, dx)
                change = A_COEF * change
                if abs(dx) <= reach:
                    change = change + at(p, dx)
                p[ob, dx + PADX, lo:hi] = change

    if own_slot:
        picked = slice(lo + rows // 2, lo + rows // 2 + rows)
    else:
        picked = pl.ds(pl.multiple_of(jnp.where(even, lo, lo + rows), SUB), rows)
    zero = jnp.zeros((rows, LANES), F32)
    blocks = nx // FINE
    shift = lax.rem(col + (nx - REACH), nx)
    depth_f = rows * nx
    total = None
    for f in range(3):
        for ob in range(nob):
            lane = slice(ob * LANES, (ob + 1) * LANES)
            fine = jnp.broadcast_to(lax.rem(shift[:, lane], FINE), (rows, LANES))
            bits = [(fine & (1 << i)) != 0 for i in range(4)]
            coarse = jnp.broadcast_to(shift[:, lane] // FINE, (FINE, LANES))
            marks = [(coarse == block).astype(F32).astype(BF16) for block in range(blocks)]
            values = [None] * (2 * FINE)
            for dx in range(-REACH, REACH + 1):
                if f == 0:
                    value = p[ob, dx + PADX, picked]
                elif abs(dx) <= REACH - 2:
                    qv, sv = qp[ob, dx + PADX, picked], sp[ob, dx + PADX, picked]
                    value = qv - CORIOLIS * sv if f == 1 else sv + CORIOLIS * qv
                elif abs(dx) == REACH - 1:
                    qv = qp[ob, dx + PADX, picked]
                    value = qv if f == 1 else CORIOLIS * qv
                else:
                    value = None
                values[dx + REACH] = value
            for i in range(4):
                moved = []
                for e in range(2 * FINE):
                    here = values[e]
                    there = values[e - (1 << i)] if e >= (1 << i) else None
                    if here is None and there is None:
                        moved.append(None)
                    else:
                        moved.append(
                            jnp.where(
                                bits[i],
                                zero if there is None else there,
                                zero if here is None else here,
                            )
                        )
                values = moved
            for e in range(2 * FINE):
                w[f, ob, e * rows : (e + 1) * rows, :] = zero if values[e] is None else values[e]
            for y in range(rows):
                both = halves(w[f, ob, pl.ds(y, 2 * FINE, stride=rows), :])
                for part, ref in zip(both, (sh, sl)):
                    near, far = part[:FINE], part[FINE:]
                    for block in range(blocks):
                        start_row = (f * rows + y) * nx + block * FINE
                        ref[start_row : start_row + FINE, lane] = (
                            near * marks[block] + far * marks[block - 1]
                        )
        span = slice(f * depth_f, (f + 1) * depth_f)
        basis = basis_ref[f]
        part = dot1(basis, sh[span, :]) + dot1(basis, sl[span, :])
        total = part if total is None else total + part
    out_ref[...] = total


def project(slot, own, first, second, basis, rows, nx):
    order = basis.shape[1]
    depth_all = 3 * rows * nx
    nobs = own.shape[1]
    nob = nobs // LANES
    wide = (nob, 2 * PADX + 1, 2 * rows + 2 * SUB, LANES)
    return pl.pallas_call(
        functools.partial(project_kernel, slot, rows, nx),
        out_shape=jax.ShapeDtypeStruct((order, nobs), F32),
        in_specs=[VMEM] * 4,
        out_specs=VMEM,
        scratch_shapes=[
            pltpu.VMEM((nob, 2 * REACH - 3, 2 * rows, LANES), F32),
            pltpu.VMEM(wide, F32),
            pltpu.VMEM(wide, F32),
            pltpu.VMEM(wide, F32),
            pltpu.VMEM(wide, F32),
            pltpu.VMEM((3, nob, 2 * FINE * rows, LANES), F32),
            pltpu.VMEM((depth_all, nobs), BF16),
            pltpu.VMEM((depth_all, nobs), BF16),
        ],
        compiler_params=params(48),
        cost_estimate=pl.CostEstimate(
            flops=4 * order * depth_all * nobs,
            bytes_accessed=2 * order * depth_all,
            transcendentals=0,
        ),
    )(own, first, second, basis)


def triangle_masks(half):
    rows = lax.broadcasted_iota(jnp.int32, (half, half), 0)
    cols = lax.broadcasted_iota(jnp.int32, (half, half), 1)
    return rows, cols


def store_packed(out_ref, matrix, vector):
    half = matrix.shape[0] // 2
    rows, cols = triangle_masks(half)
    corner = matrix[half:, half:]
    out_ref[0:half] = jnp.where(rows >= cols, matrix[:half, :half], corner)
    out_ref[half : 2 * half] = matrix[half:, :half]
    diagonal = jnp.sum(jnp.where(rows == cols, corner, 0.0), axis=0, keepdims=True)
    tail = jnp.concatenate(
        [vector[:, :half], vector[:, half:], diagonal, jnp.zeros((SUB - 3, half), F32)], axis=0
    )
    out_ref[2 * half : 2 * half + SUB] = tail


def load_packed(values):
    half = values.shape[1]
    rows, cols = triangle_masks(half)
    mixed = values[0:half]
    cross = values[half : 2 * half]
    vector = jnp.concatenate(
        [values[2 * half : 2 * half + 1], values[2 * half + 1 : 2 * half + 2]], axis=1
    )
    diagonal = values[2 * half + 2 : 2 * half + 3]
    turned = mixed.T
    first = jnp.where(rows >= cols, mixed, turned)
    last = jnp.where(rows == cols, diagonal, jnp.where(rows < cols, mixed, turned))
    top = jnp.concatenate([first, cross.T], axis=1)
    bottom = jnp.concatenate([cross, last], axis=1)
    return jnp.concatenate([top, bottom], axis=0), vector


def with_row(matrix, row):
    return jnp.concatenate([matrix, jnp.broadcast_to(row, (SUB, row.shape[1]))], axis=0)


def gram_kernel(own_ref, first_ref, second_ref, weight_ref, innovation_ref, out_ref):
    tile, tiles = lax.axis_index("tile"), lax.axis_size("tile")
    inner = (tile != 0) & (tile != tiles - 1)
    projected = own_ref[...] + first_ref[...] + jnp.where(inner, second_ref[...], 0.0)
    weight = weight_ref[...]
    left = with_row(projected * weight, weight * innovation_ref[...])
    result = dot3(halves(left), halves(projected), NT)
    size = projected.shape[0]
    store_packed(out_ref, result[:size], result[size : size + 1])


def gram(own, first, second, weight, innovation):
    order = own.shape[0]
    return pl.pallas_call(
        gram_kernel,
        out_shape=jax.ShapeDtypeStruct((order + SUB, order // 2), F32),
        in_specs=[VMEM] * 5,
        out_specs=VMEM,
        compiler_params=params(8),
        name="gram",
    )(own, first, second, weight, innovation)


def identity_like(matrix):
    rows = lax.broadcasted_iota(jnp.int32, matrix.shape, 0)
    cols = lax.broadcasted_iota(jnp.int32, matrix.shape, 1)
    return (rows == cols).astype(F32)


def norm_of(matrix):
    sums = jnp.sum(jnp.abs(matrix), axis=0, keepdims=True)
    return jnp.broadcast_to(jnp.max(sums, axis=1, keepdims=True), sums.shape)


def scaled(error):
    square = error * error
    rho = 2.0 / (2.0 - square)
    return rho, 0.5 * square * rho


def chebyshev_start(matrix, square, eye):
    bound = jnp.sqrt(norm_of(square))
    alpha = 2.0 / (2.0 + bound)
    error0 = 0.5 * bound * alpha
    rho, error = scaled(error0)
    rest = 1.0 - alpha
    factor = rho * alpha
    residual = rho * (
        (rest * rest) * eye - (2.0 * rest * alpha) * matrix + (alpha * alpha) * square
    ) - error * eye
    return factor * (2.0 - alpha), factor * alpha, residual, error, bound


def rough_turns(state, eye):
    size = eye.shape[0]
    new = []
    for estimate, residual, error in state:
        rho, error = scaled(error)
        part = residual.astype(BF16)
        moved = dot1(jnp.concatenate([estimate.astype(BF16), part], axis=0), part)
        new.append((rho * (estimate + moved[:size]), rho * moved[size:] - error * eye, error))
    return new


def polish(matrix, part, estimate, eye, exact):
    pieces = halves(estimate)
    moved = dot6(matrix, estimate) if exact else dot3(part, pieces)
    residual = eye - estimate - moved
    rough = residual.astype(BF16)
    change = residual + dot1(rough, rough)
    return estimate + dot3(pieces, halves(change))


def invert_any(matrix, part, c0, c1, error, eye):
    def unsure(state):
        return jnp.max(state[1]) > 0.03

    def turn(state):
        estimate, error = state
        pieces = halves(estimate)
        residual = 2.0 * eye - estimate - dot3(part, pieces)
        rho, error = scaled(error)
        return rho * dot3(pieces, halves(residual)), error

    estimate, error = lax.while_loop(unsure, turn, (c0 * eye - c1 * matrix, error))
    return lax.fori_loop(
        0, 4, lambda index, value: polish(matrix, part, value, eye, True), estimate
    )


def invert_shifted(matrices, parts, turns):
    eye = identity_like(matrices[0])
    state, starts, bounds = [], [], []
    for matrix, part in zip(matrices, parts):
        square = dot1(part[0], part[0])
        c0, c1, residual, error, bound = chebyshev_start(matrix, square, eye)
        state.append((c0 * eye - c1 * matrix, residual, error))
        starts.append((c0, c1, error))
        bounds.append(bound)
    narrow = jnp.max(functools.reduce(jnp.maximum, bounds)) < NARROW
    for _ in range(turns):
        state = rough_turns(state, eye)
    last = functools.reduce(jnp.maximum, [one[2] for one in state])
    enough = narrow & (jnp.max(last) < 0.04)
    quick = tuple(
        polish(m, part, one[0], eye, False) for m, part, one in zip(matrices, parts, state)
    )

    def careful():
        return tuple(
            invert_any(m, part, *start, eye) for m, part, start in zip(matrices, parts, starts)
        )

    return lax.cond(enough, lambda: quick, careful)


def solve_shifted(matrix, parts, row):
    eye = identity_like(matrix)
    row_parts = halves(row)
    extended = tuple(jnp.concatenate(two, axis=0) for two in zip(row_parts, parts))
    squares = dot3(extended, parts)
    moved, square = squares[:SUB], squares[SUB:]
    c0, c1, residual, error, _ = chebyshev_start(matrix, square, eye)
    rho, last = scaled(error)
    part = halves(residual)
    start = c0 * row - c1 * moved
    both = tuple(jnp.concatenate(two, axis=0) for two in zip(halves(start), part))
    moved = dot3(both, part)
    current = rho * (start + moved[:SUB])
    part = halves(rho * moved[SUB:] - last * eye)
    once = tile_dot(current, part)
    quick = current + once + tile_dot(once, part)

    def careful():
        inverse = invert_any(matrix, parts, c0, c1, error, eye)
        pieces = halves(inverse)

        def correct(index, value):
            miss = row - value - dot6(value, matrix)
            return value + dot3(halves(miss), pieces)

        return lax.fori_loop(0, 3, correct, dot3(row_parts, pieces))

    return lax.cond(jnp.max(last) < 0.03, lambda: quick, careful)


def column(row):
    size = row.shape[1]
    return jnp.broadcast_to(row, (size, size)).T


def moves_and_maps(transition_ref, model_error_ref):
    moves = jnp.where(lax.axis_index("tm") < 2, 0.0, 1.0)
    weighted = transition_ref[...] / column(model_error_ref[...])
    return moves, halves(weighted), halves(weighted.T)


def pair_kernel(
    full, mine_ref, other_ref, transition_ref, model_error_ref,
    prefix_ref, c1_ref, a2_ref, inverse_ref, vec_ref, *more,
):
    lower_core = lax.rem(lax.axis_index("tm"), 2) == 0
    mine, other = mine_ref[...], other_ref[...]
    q2 = model_error_ref[...]
    size = q2.shape[1]
    root_row = jnp.sqrt(q2)
    root_col = column(root_row)
    transition = transition_ref[...]
    _, weighted, turned = moves_and_maps(transition_ref, model_error_ref)
    mats, rows = [], []
    for packed in (jnp.where(lower_core, mine, other), jnp.where(lower_core, other, mine)):
        matrix, vector = load_packed(packed)
        mats.append(root_col * matrix * root_row)
        rows.append(root_row * vector)
    p1, p2 = invert_shifted(mats, [halves(m) for m in mats], 2)
    c1, c2 = root_col * p1 * root_row, root_col * p2 * root_row
    low = halves(c1)
    a2 = dot3(halves(c2), weighted)
    k1 = dot3(low, turned)
    rest2 = halves(transition - a2)
    crossed = dot3(halves(k1), rest2)
    b1 = row_dot(rows[0], halves(p1)) * root_row
    b2 = row_dot(rows[1], halves(p2)) * root_row
    a2_parts = halves(a2)
    outer = halves(dot3(low, a2_parts, NT))
    ahead = row_dot(b1, a2_parts, NT) + b2
    behind = row_dot(b2, weighted) - row_dot(row_dot(b1, turned), rest2)
    (inverse,) = invert_shifted([crossed], [halves(crossed)], 1)
    parts = halves(inverse)
    cov = dot3(a2_parts, halves(dot3(parts, outer))) + c2
    s = row_dot(behind, parts)
    mean = row_dot(s, outer) + ahead
    store_packed(prefix_ref, cov, mean)
    c1_ref[...] = c1
    a2_ref[...] = a2
    inverse_ref[...] = inverse
    vec_ref[0:1] = b1
    vec_ref[1:2] = s
    vec_ref[2:3] = mean
    vec_ref[3:SUB] = jnp.zeros((SUB - 3, size), F32)
    if full:
        more[0][...] = cov


def rest_kernel(
    full, c1_ref, a2_ref, inverse_ref, given_ref, transition_ref, model_error_ref,
    a_ref, j_ref, vec_ref, *more,
):
    lower_core = lax.rem(lax.axis_index("tm"), 2) == 0
    transition = transition_ref[...]
    moves, weighted, turned = moves_and_maps(transition_ref, model_error_ref)
    b1, s, mean = given_ref[0:1], given_ref[1:2], given_ref[2:3]
    a1 = moves * dot3(halves(c1_ref[...]), weighted)
    eta1 = moves * row_dot(b1, weighted)
    j2 = dot3(turned, halves(transition - a2_ref[...]))
    j1 = moves * dot3(turned, halves(transition - a1))
    a1_parts = halves(a1)
    spread = dot3(halves(a1.T), halves(j2))
    right = halves(dot3(halves(inverse_ref[...]), a1_parts))
    trans = dot3(halves(a2_ref[...]), right)
    prec = dot3(halves(spread), right) + j1
    info = row_dot(s, a1_parts) + eta1
    a_ref[...] = jnp.where(lower_core, a1, trans)
    j_ref[...] = jnp.where(lower_core, j1, prec)
    vec_ref[0:1] = jnp.where(lower_core, b1, mean)
    vec_ref[1:2] = jnp.where(lower_core, eta1, info)
    vec_ref[2:3] = mean
    vec_ref[3:4] = info
    vec_ref[4:SUB] = jnp.zeros((SUB - 4, mean.shape[1]), F32)
    if full:
        more[0][...] = trans
        more[1][...] = prec


def pair_up(mine, other, transition, model_error, full):
    order = transition.shape[0]
    square = jax.ShapeDtypeStruct((order, order), F32)
    rows = jax.ShapeDtypeStruct((SUB, order), F32)
    shapes = [jax.ShapeDtypeStruct(mine.shape, F32), square, square, square, rows]
    shapes = shapes + [square] * (1 if full else 0)
    return pl.pallas_call(
        functools.partial(pair_kernel, full),
        out_shape=shapes,
        in_specs=[VMEM] * 4,
        out_specs=[VMEM] * len(shapes),
        compiler_params=params(24),
        name="pair_up",
    )(mine, other, transition, model_error)


def pair_rest(c1, a2, inverse, given, transition, model_error, full):
    order = transition.shape[0]
    square = jax.ShapeDtypeStruct((order, order), F32)
    rows = jax.ShapeDtypeStruct((SUB, order), F32)
    shapes = [square, square, rows] + [square] * (2 if full else 0)
    return pl.pallas_call(
        functools.partial(rest_kernel, full),
        out_shape=shapes,
        in_specs=[VMEM] * 6,
        out_specs=[VMEM] * len(shapes),
        compiler_params=params(24),
        name="pair_rest",
    )(c1, a2, inverse, given, transition, model_error)


def advance_kernel(incoming_ref, a_ref, j_ref, c_ref, vec_ref, out_ref):
    cov0, mean0 = load_packed(incoming_ref[...])
    low = halves(cov0)
    forward = halves(a_ref[...])
    back = halves(j_ref[...])
    crossed = dot3(low, back)
    outer = halves(dot3(low, forward, NT))
    behind = vec_ref[3:4] - row_dot(mean0, back)
    (inverse,) = invert_shifted([crossed], [halves(crossed)], 1)
    inverse = halves(inverse)
    s = row_dot(behind, inverse)
    mean = row_dot(mean0, forward, NT) + row_dot(s, outer) + vec_ref[2:3]
    cov = dot3(forward, halves(dot3(inverse, outer))) + c_ref[...]
    store_packed(out_ref, cov, mean)


def advance_prefix(incoming, a, j, c, vec):
    return pl.pallas_call(
        advance_kernel,
        out_shape=jax.ShapeDtypeStruct(incoming.shape, F32),
        in_specs=[VMEM] * 5,
        out_specs=VMEM,
        compiler_params=params(16),
        name="advance_prefix",
    )(incoming, a, j, c, vec)


def finish_kernel(rows, nx, incoming_ref, a_ref, j_ref, vec_ref, basis_ref, mean_ref, sum_ref):
    moves = jnp.where(lax.axis_index("tm") < 2, 0.0, 1.0)
    cov0, mean0 = load_packed(incoming_ref[...] * moves)
    size = mean0.shape[1]
    low = halves(with_row(cov0, mean0))
    crossed = dot3(low, halves(j_ref[...]))
    outer = dot3(low, halves(a_ref[...]), NT)
    matrix = crossed[:size]
    target = jnp.broadcast_to(vec_ref[1:2], (SUB, size)) - crossed[size:]
    s = solve_shifted(matrix, halves(matrix), target)
    mean = (tile_dot(s, halves(outer[:size])) + outer[size:] + vec_ref[0:1])[0:1]
    mean_ref[...] = mean
    pieces = jnp.concatenate(list(thirds(mean)) + [jnp.zeros((5, size), BF16)], axis=0)
    for f in range(3):
        sums = dot1(pieces, basis_ref[f])
        total = sums[0:1] + (sums[1:2] + sums[2:3])
        for y in range(rows):
            i = f * rows + y
            sum_ref[i : i + 1, :] = total[:, y * nx : (y + 1) * nx]


def finish(incoming, a, j, vec, basis, rows, nx):
    order = a.shape[0]
    return pl.pallas_call(
        functools.partial(finish_kernel, rows, nx),
        out_shape=[
            jax.ShapeDtypeStruct((1, order), F32),
            jax.ShapeDtypeStruct((3 * rows, nx), F32),
        ],
        in_specs=[VMEM] * 5,
        out_specs=[VMEM] * 2,
        compiler_params=params(16),
        name="finish",
    )(incoming, a, j, vec, basis)


def increments_kernel(rows, nx, own_ref, first_ref, second_ref, mo, mf, ms, out_ref):
    tile, tiles = lax.axis_index("tile"), lax.axis_size("tile")

    def extend(own, first, second):
        before, after = before_after(first, second)
        return jnp.concatenate([before, own, after], axis=0)

    depth = extend(mo[0:rows, :], mf[0:rows, :], ms[0:rows, :]) * B_COEF
    h, u, v = [
        extend(*(ref[f * rows : (f + 1) * rows, :] for ref in (own_ref, first_ref, second_ref)))
        for f in range(3)
    ]
    total = 3 * rows
    y_iota = lax.broadcasted_iota(jnp.int32, (total, nx), 0)
    first_row = jnp.where(tile == 0, rows, 0)
    last_row = jnp.where(tile == tiles - 1, 2 * rows, total)
    inside = ((y_iota >= first_row) & (y_iota < last_row)).astype(F32)

    def cols(values, by):
        return pltpu.roll(values, by % nx, 1)

    def lines(values, by):
        return pltpu.roll(values, by % total, 0)

    after, before = lines(inside, -1), lines(inside, 1)
    for _ in range(STEPS):
        east, north = u + CORIOLIS * v, v - CORIOLIS * u
        slope_cols = cols(east, -1) - cols(east, 1) - A_COEF * (
            (cols(h, -2) - h) - (h - cols(h, 2))
        )
        slope_lines = after * (lines(north, -1) - A_COEF * (lines(h, -2) - h)) - before * (
            lines(north, 1) - A_COEF * (h - lines(h, 2))
        )
        u = east - A_COEF * (cols(h, -1) - cols(h, 1))
        v = inside * (north - A_COEF * (lines(h, -1) - lines(h, 1)))
        h = h - depth * (slope_cols + slope_lines)
    for f, values in enumerate((h, u, v)):
        out_ref[f] = values[rows : 2 * rows]


def propagate_sum(own, first, second, mo, mf, ms, rows, nx):
    return pl.pallas_call(
        functools.partial(increments_kernel, rows, nx),
        out_shape=jax.ShapeDtypeStruct((3, rows, nx), F32),
        in_specs=[VMEM] * 6,
        out_specs=VMEM,
        compiler_params=params(8),
        name="propagate_sum",
    )(own, first, second, mo, mf, ms)


def layout_kernel(fields_ref, out_ref, held, sems, *spread):
    count, order, rows, nx = fields_ref.shape
    copies = [
        pltpu.make_async_copy(fields_ref.at[f], held.at[f], sems.at[f]) for f in range(count)
    ]
    for copy in copies:
        copy.start()
    for f, copy in enumerate(copies):
        copy.wait()
        for ob, ref in enumerate(spread):
            lane = slice(ob * LANES, (ob + 1) * LANES)
            ref[...] = held[f, :, :, lane].astype(F32).reshape(order * rows, LANES)
            for y in range(rows):
                start = y * nx + ob * LANES
                out_ref[f, :, start : start + LANES] = ref[
                    pl.ds(y, order, stride=rows), :
                ].astype(BF16)


def lay_out(fields):
    count, order, rows, nx = fields.shape
    return pl.pallas_call(
        layout_kernel,
        out_shape=jax.ShapeDtypeStruct((count, order, rows * nx), BF16),
        in_specs=[pl.BlockSpec(memory_space=pl.ANY)],
        out_specs=VMEM,
        scratch_shapes=[pltpu.VMEM(fields.shape, BF16), pltpu.SemaphoreType.DMA((count,))]
        + [pltpu.VMEM((order * rows, LANES), F32)] * (nx // LANES),
        compiler_params=params(50),
        name="lay_out",
    )(fields)


def info_kernel(depth_ref, cells_ref, fields_ref, out_ref, cells, fields, sems):
    rows = depth_ref.shape[0]
    copies = [
        pltpu.make_async_copy(source, target, sems.at[i])
        for i, (source, target) in enumerate((
            (depth_ref, out_ref.at[0:rows]), (cells_ref, cells), (fields_ref, fields),
        ))
    ]
    for copy in copies:
        copy.start()
    out_ref[rows : 2 * rows, :] = jnp.zeros(depth_ref.shape, F32)
    for copy in copies:
        copy.wait()
    out_ref[rows : rows + 1, :] = cells[...].astype(F32)
    out_ref[rows + 1 : rows + 2, :] = fields[...].astype(F32)


def gather_info(mean_depth, obs_cells, obs_fields):
    rows, nx = mean_depth.shape
    return pl.pallas_call(
        info_kernel,
        out_shape=jax.ShapeDtypeStruct((2 * rows, nx), F32),
        in_specs=[pl.BlockSpec(memory_space=pl.ANY)] * 3,
        out_specs=VMEM,
        scratch_shapes=[
            pltpu.VMEM(obs_cells.shape, jnp.int32),
            pltpu.VMEM(obs_fields.shape, jnp.int32),
            pltpu.SemaphoreType.DMA((3,)),
        ],
        compiler_params=params(60),
        name="gather_info",
    )(mean_depth, obs_cells, obs_fields)


def on_device(
    basis_fields, mean_depth, obs_cells, obs_fields, obs_weight, innovation, transition, model_error
):
    _, rows, nx = basis_fields.shape[2:]
    tiles = lax.axis_size("tile")
    windows = lax.axis_size("tm")
    near = [(i, i ^ 1) for i in range(tiles)]
    across = [i if i in (0, tiles - 1) else (i + 1 if i % 2 else i - 1) for i in range(tiles)]
    far = [
        (w * tiles + i, (w ^ 1 if across[i] == i else w) * tiles + across[i])
        for w in range(windows)
        for i in range(tiles)
    ]

    def swap_near(array):
        return lax.ppermute(array, "tile", near)

    def swap_far(array):
        return lax.ppermute(array, ("tm", "tile"), far)

    info = gather_info(mean_depth, obs_cells, obs_fields)
    info_near = swap_near(info)
    info_far = swap_far(info)
    basis = lay_out(basis_fields[0])

    part_near = project(NEAR, info, info_near, info_near, basis, rows, nx)
    got_near = swap_near(part_near)
    info_far, unused = lax.optimization_barrier((info_far, part_near))
    part_far = project(FAR, info, info_far, info_far, basis, rows, nx)
    got_far = swap_far(part_far)
    info_own, unused = lax.optimization_barrier((info, part_far))
    part_own = project(OWN, info_own, info_near, info_far, basis, rows, nx)

    packed = gram(part_own, got_near, got_far, obs_weight, innovation)
    bit = 1
    while bit < tiles:
        reach = 3 if bit * 2 < tiles else 1
        parts = [
            lax.ppermute(packed, "tile", [(i, i ^ (bit * by)) for i in range(tiles)])
            for by in range(1, reach + 1)
        ]
        packed = packed + parts[0]
        if reach == 3:
            packed = packed + (parts[1] + parts[2])
        bit *= reach + 1
    other = lax.ppermute(packed, "tm", [(i, i ^ 1) for i in range(windows)])
    pairs = windows // 2
    full = pairs > 2
    errors = model_error[None, :]
    prefix, c1, a2, inverse, given, *covs = pair_up(packed, other, transition, errors, full)
    a, j, vec, *wide = pair_rest(c1, a2, inverse, given, transition, errors, full)
    incoming = jnp.zeros_like(prefix)
    pair = lax.axis_index("tm") // 2
    for turn in range(pairs - 1):
        if pairs == 2:
            hop = [(i, i ^ 2) for i in range(windows)]
        else:
            hop = [(i, i + 2) for i in range(windows - 2)]
        incoming = lax.ppermute(prefix, "tm", hop)
        if turn < pairs - 2:
            longer = advance_prefix(incoming, *wide, *covs, vec)
            prefix = jnp.where(pair == turn + 1, longer, prefix)
    mean, sums = finish(incoming, a, j, vec, basis, rows, nx)
    sums_near = swap_near(sums)
    sums_far = swap_far(sums)
    result = propagate_sum(sums, sums_near, sums_far, info, info_near, info_far, rows, nx)
    return mean, result[None]


def solution(mesh):
    return jax.shard_map(
        on_device,
        mesh=mesh,
        in_specs=(
            P("tm", None, None, "tile", None),
            P("tile", None),
            P("tm", "tile"),
            P("tm", "tile"),
            P("tm", "tile"),
            P("tm", "tile"),
            P(),
            P(),
        ),
        out_specs=(P("tm", None), P("tm", None, "tile", None)),
        check_vma=False,
    )
```
